32 devices in a mesh: node: 8 (over z, core), local: 4 (over y, x).
Axes of the slice: x: 2, y: 2, z: 4, core: 2. Of those that a mesh axis runs over, the one named last changes fastest.
Arguments:
- images: float32 [256, 7, 7, 512], P(('node', 'local')), may hold values from -11 to 11, as said below
- targets: float32 [256, 7, 7, 512], P(('node', 'local')), may hold values from -6 to 6
- weight: float32 [3, 3, 512, 512], replicated, may hold values from -0.09375 to 0.09375
Outputs:
- combined: float32 [4608, 512], P('local', 'node')
The draws below stay inside these ranges and needn't reach their ends.
Inputs may be any that keep to these rules, and one draw needn't show every extreme that they name: `images`: entries are real-valued, of order one.
All inputs are finite; a program needn't handle non-finite values.
Results may differ from the reference program's by a relative error of at most 0.00013.
Values sent between devices are 32-bit elements; how exact they have to be, the bound alone decides.
No kernel may reach another device: no remote copies, remote signals or barrier semaphores. Data moves between devices by JAX's collectives and lax.ppermute only.
A program may use at most 128 MiB of HBM per device.

```python
import jax
import jax.numpy as jnp
from jax import lax

C = 512
SIDE = 7
IMG_DEV = 8
IMAGES = 256
N_NODE = 8
N_LOCAL = 4


def draw_images(key, part):
    key_base, key_jitter = jax.random.split(jax.random.fold_in(key, 7101), 2)
    shape = (IMAGES, SIDE, SIDE, C)
    base = jnp.clip(jax.random.normal(key_base, shape, jnp.float32), -5.0, 5.0)
    position = jnp.arange(IMAGES, dtype=jnp.float32) / max(IMAGES - 1, 1)
    rising = jnp.exp((position - 0.5) * jnp.log(3.0))
    jitter = jnp.exp(jax.random.uniform(key_jitter, (IMAGES,), jnp.float32, jnp.log(0.8), jnp.log(1.25)))
    factor = (rising * jitter)[:, None, None, None]
    return (base * factor).astype(jnp.float32)


def block_levels(stream_key, dims, shards, low, top_value):
    level, own = 1.0, jax.random.fold_in(stream_key, 6)
    for dim, shards_of in shards:
        steps = jnp.exp(jax.random.uniform(jax.random.fold_in(own, dim), (shards_of,), jnp.float32, low / len(shards), top_value / len(shards)))
        level = level * jnp.repeat(steps, dims[dim] // shards_of).reshape([-1 if axis == dim else 1 for axis in range(len(dims))])
    return level


def noise(own_key, extent, spread, most, cuts=(), kind=jnp.bfloat16):
    loudness = block_levels(own_key, extent, cuts, -0.22, 0.18) if cuts else 1.0
    entries = jax.random.normal(own_key, extent, jnp.float32) * spread * loudness
    return jnp.minimum(jnp.maximum(entries, -most), most).astype(kind)


def setup_inputs(seed: int = 0) -> dict:
    splits = jax.random.split(jax.random.key(seed), 4)
    images = draw_images(jax.random.fold_in(splits[3], 71), 0)
    targets = noise(splits[1], (IMAGES, SIDE, SIDE, C), 1.0, 6.0, ((0, 32),), jnp.float32)
    weight = noise(splits[2], (3, 3, C, C), (9 * C) ** -0.5, 0.09375, (), jnp.float32)
    return dict(images=images, targets=targets, weight=weight)


epsilon = 1e-6


def make_patches(images):
    padded = jnp.pad(images, ((0, 0), (1, 1), (1, 1), (0, 0)))
    tap_views = []
    for row_shift in range(3):
        for col_shift in range(3):
            tap_views.append(padded[:, row_shift:row_shift + SIDE, col_shift:col_shift + SIDE, :])
    joined = jnp.concatenate(tap_views, axis=-1)
    return joined.reshape(-1, 9 * images.shape[3])


def reference(images, targets, weight):
    flat_w = weight.reshape(9 * C, C)
    node_images = images.reshape(N_NODE, N_LOCAL * IMG_DEV, SIDE, SIDE, C)
    node_targets = targets.reshape(N_NODE, N_LOCAL * IMG_DEV * SIDE * SIDE, C)

    def per_node(pair):
        patches = make_patches(pair[0])
        outputs = jnp.dot(patches, flat_w, precision=lax.Precision.HIGHEST, preferred_element_type=jnp.float32)
        residual = outputs - pair[1]
        gradient = lax.dot_general(patches, residual, (((0,), (0,)), ((), ())), precision=lax.Precision.HIGHEST, preferred_element_type=jnp.float32)
        return gradient * (1.0 / (IMG_DEV * SIDE * SIDE))

    grads = lax.map(per_node, (node_images, node_targets))
    node_ids = jnp.arange(N_NODE, dtype=jnp.int32)
    levels = N_NODE.bit_length() - 1
    for tree_level in range(levels):
        partner_ids = jnp.bitwise_xor(node_ids, jnp.int32(1 << tree_level))
        partner_grads = grads[partner_ids]
        is_upper = (jnp.bitwise_and(jnp.right_shift(node_ids, tree_level), 1) == 1)[:, None, None]
        left_vec = jnp.where(is_upper, partner_grads, grads)
        right_vec = jnp.where(is_upper, grads, partner_grads)
        cross_sum = jnp.sum(left_vec * right_vec, axis=(1, 2), keepdims=True)
        left_sq = jnp.sum(left_vec * left_vec, axis=(1, 2), keepdims=True)
        right_sq = jnp.sum(right_vec * right_vec, axis=(1, 2), keepdims=True)
        grads = (1.0 - cross_sum / (2.0 * (left_sq + epsilon))) * left_vec + (1.0 - cross_sum / (2.0 * (right_sq + epsilon))) * right_vec
    return grads[0]
```

```python
import jax
import jax.numpy as jnp
from jax import lax
from jax.experimental import pallas as pl
from jax.experimental.pallas import tpu as pltpu
from jax.sharding import PartitionSpec as P

epsilon = 1e-06
HALF = 64
BLK = 32


def partner(value, axis, distance):
    mask = 2**distance
    pairs = [(source, source ^ mask) for source in range(lax.axis_size(axis))]
    return lax.ppermute(value, axis, pairs)


def make_patches(images):
    side = images.shape[1]
    padded = jnp.pad(images, ((0, 0), (1, 1), (1, 1), (0, 0)))
    tap_views = []
    for row_shift in range(3):
        for col_shift in range(3):
            tap_views.append(padded[:, row_shift : row_shift + side, col_shift : col_shift + side, :])
    joined = jnp.concatenate(tap_views, axis=-1)
    return joined.reshape(-1, 9 * images.shape[3])


def adasum_pair(left_vec, right_vec, cross_sum, left_sq, right_sq):
    left_coef = 1.0 - cross_sum / (2.0 * (left_sq + epsilon))
    right_coef = 1.0 - cross_sum / (2.0 * (right_sq + epsilon))
    return left_coef * left_vec + right_coef * right_vec


def general_plan(images, targets, weight):
    channels = images.shape[3]
    flat_w = weight.reshape(9 * channels, channels)
    patches = make_patches(images)
    outputs = jnp.dot(patches, flat_w, precision=lax.Precision.HIGHEST, preferred_element_type=jnp.float32)
    residual = outputs - targets.reshape(-1, channels)
    row_scale = 1.0 / patches.shape[0]
    product = lax.dot_general(
        patches,
        residual,
        (((0,), (0,)), ((), ())),
        precision=lax.Precision.HIGHEST,
        preferred_element_type=jnp.float32,
    )
    my_rows = lax.psum_scatter(product * row_scale, "local", scatter_dimension=0, tiled=True)
    node_count = lax.axis_size("node")
    levels = node_count.bit_length() - 1
    row_count = my_rows.shape[0]
    col_width = channels // node_count
    node_id = lax.axis_index("node")
    piece_blocks = my_rows.reshape(row_count, node_count, col_width)
    for tree_level in range(levels):
        is_upper = jnp.bitwise_and(jnp.right_shift(node_id, tree_level), 1) == 1
        remaining = piece_blocks.shape[1]
        split_view = piece_blocks.reshape(row_count, remaining // 2, 2, col_width)
        lower_half = split_view[:, :, 0, :]
        upper_half = split_view[:, :, 1, :]
        kept_part = jnp.where(is_upper, upper_half, lower_half)
        sent_part = jnp.where(is_upper, lower_half, upper_half)
        received = partner(sent_part, "node", tree_level)
        first_part = jnp.where(is_upper, received, kept_part)
        second_part = jnp.where(is_upper, kept_part, received)
        totals = jnp.stack(
            [
                jnp.sum(first_part * second_part),
                jnp.sum(first_part * first_part),
                jnp.sum(second_part * second_part),
            ]
        )
        totals = lax.psum(totals, "local")
        for inner_bit in range(tree_level + 1):
            totals = totals + partner(totals, "node", inner_bit)
        piece_blocks = adasum_pair(first_part, second_part, totals[0], totals[1], totals[2])
    return piece_blocks.reshape(row_count, col_width)


def hop(value, mapping):
    z_count = lax.axis_size("node") // 2
    pairs = []
    for z in range(z_count):
        for c in range(2):
            for y in range(2):
                for x in range(2):
                    tz, tc, ty, tx = mapping(z, c, y, x)
                    pairs.append((((z * 2 + c) * 2 + y) * 2 + x, ((tz * 2 + tc) * 2 + ty) * 2 + tx))
    return lax.ppermute(value, ("node", "local"), pairs)


def split2(v):
    hi = v.astype(jnp.bfloat16)
    lo = (v - hi.astype(jnp.float32)).astype(jnp.bfloat16)
    return hi, lo


def mm(a, b):
    return jnp.dot(a, b, preferred_element_type=jnp.float32)


def low_lanes(shape):
    return lax.broadcasted_iota(jnp.int32, shape, len(shape) - 1) < HALF


def pair_pack(a, b):
    low = low_lanes(a.shape)
    axis = a.ndim - 1
    return (jnp.where(low, a, pltpu.roll(b, HALF, axis)), jnp.where(low, pltpu.roll(a, HALF, axis), b))


def lane_halves(v):
    evens, odds = [], []
    for k in range(v.shape[1] // 256):
        e, o = pair_pack(v[:, 256 * k : 256 * k + 128], v[:, 256 * k + 128 : 256 * k + 256])
        evens.append(e)
        odds.append(o)
    return jnp.concatenate(evens, axis=1), jnp.concatenate(odds, axis=1)


def split_kernel(s_ref, x_ref, own_ref, other_ref):
    even, odd = lane_halves(x_ref[...])
    up = s_ref[0] == 1
    own_ref[...] = jnp.where(up, odd, even)
    other_ref[...] = jnp.where(up, even, odd)


def residual_kernel(s_ref, x_ref, t_ref, w_ref, own_ref, other_ref, pad_ref, acc_ref):
    side = x_ref.shape[0]
    imgs, ch = x_ref.shape[2], x_ref.shape[3]
    rows = side * side * imgs
    tap = pl.program_id(0)

    @pl.when(tap == 0)
    def _():
        pad_ref[...] = jnp.zeros(pad_ref.shape, jnp.float32)
        pad_ref[1 : side + 1, 1 : side + 1] = x_ref[...]
        acc_ref[...] = -t_ref[...]

    shifted = pad_ref[pl.ds(tap // 3, side), pl.ds(tap % 3, side)].reshape(rows, ch)
    xh, xl = split2(shifted)
    wh, wl = split2(w_ref[0])
    acc_ref[...] += mm(xh, wh) + (mm(xh, wl) + mm(xl, wh))

    @pl.when(tap == pl.num_programs(0) - 1)
    def _():
        even, odd = lane_halves(acc_ref[...])
        up = s_ref[0] == 1
        own_ref[...] = jnp.where(up, odd, even)
        other_ref[...] = jnp.where(up, even, odd)


def gradient_kernel(
    scale, side, s_ref, x0, x1, x2, x3, r0, r1, r2, r3, keep_ref, send_ref, xth, xtl, rh, rl, g_ref
):
    xs, rs = (x0, x1, x2, x3), (r0, r1, r2, r3)
    rows, width = x0.shape
    strip = rows // side
    imgs = strip // side
    zero = jnp.zeros((side, 1, 4 * imgs, width), jnp.bfloat16)
    for ref in (rh, rl):
        ref[:, 0:1] = zero
        ref[:, side + 1 : side + 2] = zero
    for r in range(side):
        def gather(refs):
            parts = [ref[r * strip : (r + 1) * strip, :].reshape(side, imgs, width) for ref in refs]
            return jnp.concatenate(parts, axis=1)

        xh, xl = split2(gather(xs).reshape(4 * strip, width).T)
        xth[r] = xh
        xtl[r] = xl
        h, lo = split2(gather(rs))
        rh[r, 1 : side + 1] = h
        rl[r, 1 : side + 1] = lo

    def column(j, carry):
        for i in range(3):
            total = None
            for r in range(side):
                p = r - i + 1
                if p < 0 or p >= side:
                    continue
                bh = rh[p, pl.ds(2 - j, side)].reshape(4 * strip, width)
                bl = rl[p, pl.ds(2 - j, side)].reshape(4 * strip, width)
                part = mm(xth[r], bh) + (mm(xth[r], bl) + mm(xtl[r], bh))
                total = part if total is None else total + part
            per = width // BLK
            g_ref[pl.ds((3 * i + j) * per, per)] = (total * scale).reshape(per, BLK, width)
        return carry

    lax.fori_loop(0, 3, column, 0)
    core = s_ref[0]
    z = s_ref[1]
    half = g_ref.shape[0] // 2
    for m in range(half // 2):
        for which, out in ((core, keep_ref), (1 - core, send_ref)):
            a = g_ref[2 * m + which]
            b = g_ref[half + 2 * m + which]
            for k in range(width // 128):
                lo, hi = pair_pack(a[:, 128 * k : 128 * k + 128], b[:, 128 * k : 128 * k + 128])
                out[jnp.bitwise_xor(2 * k, z), m * BLK : (m + 1) * BLK, :] = lo
                out[jnp.bitwise_xor(2 * k + 1, z), m * BLK : (m + 1) * BLK, :] = hi


def finish_kernel(s_ref, f_ref, s0, s1, s2, s3, o0, o1, o2, o3, buf):
    total = f_ref[0] * s0[...] + f_ref[1] * s1[...] + (f_ref[2] * s2[...] + f_ref[3] * s3[...])
    rows = total.shape[0] // 2
    buf[...] = total.reshape(2, rows, total.shape[1])
    core, y = s_ref[0], s_ref[1]
    for dx in range(2):
        block = buf[jnp.bitwise_xor(core, dx)]
        first, second = pair_pack(block[: rows // 2], block[rows // 2 :])
        for dy, out in ((0, (o0, o1)[dx]), (1, (o2, o3)[dx])):
            out[...] = jnp.where(jnp.bitwise_xor(y, dy) == 1, second, first)


def place_kernel(s_ref, b0, b1, b2, b3, out_ref):
    x, y = s_ref[0], s_ref[1]
    for index, ref in enumerate((b0, b1, b2, b3)):
        dy, dx = index // 2, index % 2
        block = ref[...]
        upper = pltpu.roll(block, HALF, 1)
        rows = jnp.concatenate([block[:, :HALF], upper[:, :HALF]], axis=0)
        rows = rows.reshape(out_ref.shape[0], BLK, HALF)
        slot = 2 * jnp.bitwise_xor(y, dy) + jnp.bitwise_xor(x, dx)
        for k in range(out_ref.shape[0]):
            out_ref[k, slot] = rows[k]


VM = pl.BlockSpec(memory_space=pltpu.VMEM)
SM = pl.BlockSpec(memory_space=pltpu.SMEM)


def f32(*shape):
    return jax.ShapeDtypeStruct(shape, jnp.float32)


def tile_plan(images, targets, weight):
    imgs, side, _, channels = images.shape
    width = channels // 2
    rows = side * side * imgs
    node_id = lax.axis_index("node")
    local_id = lax.axis_index("local")
    z, c = node_id // 2, node_id % 2
    y, x = local_id // 2, local_id % 2

    def scalars(*values):
        return jnp.stack([jnp.asarray(v, jnp.int32) for v in values])

    xt = jnp.transpose(images, (1, 2, 0, 3))
    x_own, x_other = pl.pallas_call(
        split_kernel,
        out_shape=(f32(rows, width), f32(rows, width)),
        in_specs=[SM, VM],
        out_specs=(VM, VM),
        name="split_images",
    )(scalars(y), xt.reshape(rows, channels))
    x_y = hop(x_other, lambda z, c, y, x: (z, c, 1 - y, x))
    x_x = hop(x_own, lambda z, c, y, x: (z, c, y, 1 - x))
    x_d = hop(x_other, lambda z, c, y, x: (z, c, 1 - y, 1 - x))

    tt = jnp.transpose(targets, (1, 2, 0, 3)).reshape(rows, channels)
    taps = weight.shape[0] * weight.shape[1]
    whole = lambda *shape: pl.BlockSpec(shape, lambda t: (0,) * len(shape))
    r_own, r_other = pl.pallas_call(
        residual_kernel,
        grid=(taps,),
        out_shape=(f32(rows, width), f32(rows, width)),
        in_specs=[
            SM,
            whole(side, side, imgs, channels),
            whole(rows, channels),
            pl.BlockSpec((1, channels, channels), lambda t: (t, 0, 0)),
        ],
        out_specs=(whole(rows, width), whole(rows, width)),
        scratch_shapes=[
            pltpu.VMEM((side + 2, side + 2, imgs, channels), jnp.float32),
            pltpu.VMEM((rows, channels), jnp.float32),
        ],
        cost_estimate=pl.CostEstimate(
            flops=6 * rows * taps * channels * channels, bytes_accessed=4 * taps * channels * channels, transcendentals=0
        ),
        name="residual",
    )(scalars(x), xt, tt, weight.reshape(taps, channels, channels))
    r_x = hop(r_other, lambda z, c, y, x: (z, c, y, 1 - x))
    r_d = hop(r_other, lambda z, c, y, x: (z, c, 1 - y, 1 - x))
    r_y = hop(r_own, lambda z, c, y, x: (z, c, 1 - y, x))

    z_count = lax.axis_size("node") // 2
    part = taps * width // 4
    keep, send = pl.pallas_call(
        lambda *refs: gradient_kernel(1.0 / rows, side, *refs),
        out_shape=(f32(z_count, part, 128), f32(z_count, part, 128)),
        in_specs=[SM] + [VM] * 8,
        out_specs=(VM, VM),
        scratch_shapes=[
            pltpu.VMEM((side, width, 4 * rows // side), jnp.bfloat16),
            pltpu.VMEM((side, width, 4 * rows // side), jnp.bfloat16),
            pltpu.VMEM((side, side + 2, 4 * imgs, width), jnp.bfloat16),
            pltpu.VMEM((side, side + 2, 4 * imgs, width), jnp.bfloat16),
            pltpu.VMEM((taps * width // BLK, BLK, width), jnp.float32),
        ],
        cost_estimate=pl.CostEstimate(
            flops=24 * rows * taps * width * width, bytes_accessed=4 * taps * width * width, transcendentals=0
        ),
        name="gradient",
    )(scalars(c, z), x_own, x_x, x_y, x_d, r_own, r_x, r_y, r_d)

    received = hop(send, lambda z, c, y, x: (z, 1 - c, y, x))
    cross, mine, theirs = jnp.sum(keep * received), jnp.sum(keep * keep), jnp.sum(received * received)
    swapped = hop(jnp.stack([cross, theirs, mine]), lambda z, c, y, x: (z, 1 - c, y, x))
    totals = jnp.stack([cross, mine, theirs]) + swapped
    totals = totals + hop(totals, lambda z, c, y, x: (z, c, y, 1 - x))
    totals = totals + hop(totals, lambda z, c, y, x: (z, c, 1 - y, x))
    keep_coef = 1.0 - totals[0] / (2.0 * (totals[1] + epsilon))
    received_coef = 1.0 - totals[0] / (2.0 * (totals[2] + epsilon))
    pieces = [keep_coef * keep[d] + received_coef * received[d] for d in range(z_count)]

    node = [pieces[0]]
    for d in range(1, z_count):
        node.append(hop(pieces[d], lambda z, c, y, x, d=d: (z ^ d, c, y, x)))
    gram = jnp.stack([jnp.stack([jnp.sum(node[min(a, b)] * node[max(a, b)]) for b in range(4)]) for a in range(4)])
    gram = gram + hop(gram, lambda z, c, y, x: (z, 1 - c, y, x))
    gram = gram + hop(gram, lambda z, c, y, x: (z, c, y, 1 - x))
    gram = gram + hop(gram, lambda z, c, y, x: (z, c, 1 - y, x))
    for bit in (1, 2):
        other = hop(gram, lambda z, c, y, x, bit=bit: (z ^ bit, c, y, x))
        order = [a ^ bit for a in range(4)]
        gram = gram + jnp.stack([jnp.stack([other[a, b] for b in order]) for a in order])
    p = [1.0 - gram[a, a ^ 1] / (2.0 * (gram[a, a] + epsilon)) for a in range(4)]
    cross = p[0] * (p[2] * gram[0, 2] + p[3] * gram[0, 3]) + p[1] * (p[2] * gram[1, 2] + p[3] * gram[1, 3])
    near = p[0] * p[0] * gram[0, 0] + 2.0 * p[0] * p[1] * gram[0, 1] + p[1] * p[1] * gram[1, 1]
    far = p[2] * p[2] * gram[2, 2] + 2.0 * p[2] * p[3] * gram[2, 3] + p[3] * p[3] * gram[3, 3]
    near_coef = 1.0 - cross / (2.0 * (near + epsilon))
    far_coef = 1.0 - cross / (2.0 * (far + epsilon))
    coefs = jnp.stack([near_coef * p[0], near_coef * p[1], far_coef * p[2], far_coef * p[3]])

    blocks = pl.pallas_call(
        finish_kernel,
        out_shape=(f32(part // 4, 128),) * 4,
        in_specs=[SM, SM] + [VM] * 4,
        out_specs=(VM,) * 4,
        scratch_shapes=[pltpu.VMEM((2, part // 2, 128), jnp.float32)],
        name="finish",
    )(scalars(c, y), coefs, *node)
    moved = []
    for index in range(4):
        dy, dx = index // 2, index % 2
        moved.append(hop(blocks[index], lambda z, c, y, x, dy=dy, dx=dx: (z, x, y ^ dy, c ^ dx)))
    out = pl.pallas_call(
        place_kernel,
        out_shape=f32(part // 2 // BLK, 4, BLK, HALF),
        in_specs=[SM] + [VM] * 4,
        out_specs=VM,
        name="place",
    )(scalars(x, y), *moved)
    return out.reshape(2 * part, HALF)


def fits(images, mesh):
    return (
        mesh.shape["local"] == 4
        and mesh.shape["node"] == 8
        and images.shape[3] == mesh.shape["node"] * HALF
        and images.shape[0] // mesh.size == 8
    )


def solution(mesh):
    def run(images, targets, weight):
        plan = tile_plan if fits(images, mesh) else general_plan
        return jax.shard_map(
            plan,
            mesh=mesh,
            in_specs=(
                P(("node", "local"), None, None, None),
                P(("node", "local"), None, None, None),
                P(),
            ),
            out_specs=P("local", "node"),
            check_vma=False,
        )(images, targets, weight)

    return run
```

```python
import jax
import jax.numpy as jnp
from jax import lax
from jax.experimental import pallas as pl
from jax.experimental.pallas import tpu as pltpu
from jax.sharding import PartitionSpec as P

epsilon = 1e-06
HALF = 64
BLK = 32


def partner(value, axis, distance):
    mask = 2**distance
    pairs = [(source, source ^ mask) for source in range(lax.axis_size(axis))]
    return lax.ppermute(value, axis, pairs)


def make_patches(images):
    side = images.shape[1]
    padded = jnp.pad(images, ((0, 0), (1, 1), (1, 1), (0, 0)))
    tap_views = []
    for row_shift in range(3):
        for col_shift in range(3):
            tap_views.append(padded[:, row_shift : row_shift + side, col_shift : col_shift + side, :])
    joined = jnp.concatenate(tap_views, axis=-1)
    return joined.reshape(-1, 9 * images.shape[3])


def adasum_pair(left_vec, right_vec, cross_sum, left_sq, right_sq):
    left_coef = 1.0 - cross_sum / (2.0 * (left_sq + epsilon))
    right_coef = 1.0 - cross_sum / (2.0 * (right_sq + epsilon))
    return left_coef * left_vec + right_coef * right_vec


def general_plan(images, targets, weight):
    channels = images.shape[3]
    flat_w = weight.reshape(9 * channels, channels)
    patches = make_patches(images)
    outputs = jnp.dot(patches, flat_w, precision=lax.Precision.HIGHEST, preferred_element_type=jnp.float32)
    residual = outputs - targets.reshape(-1, channels)
    row_scale = 1.0 / patches.shape[0]
    product = lax.dot_general(
        patches,
        residual,
        (((0,), (0,)), ((), ())),
        precision=lax.Precision.HIGHEST,
        preferred_element_type=jnp.float32,
    )
    my_rows = lax.psum_scatter(product * row_scale, "local", scatter_dimension=0, tiled=True)
    node_count = lax.axis_size("node")
    levels = node_count.bit_length() - 1
    row_count = my_rows.shape[0]
    col_width = channels // node_count
    node_id = lax.axis_index("node")
    piece_blocks = my_rows.reshape(row_count, node_count, col_width)
    for tree_level in range(levels):
        is_upper = jnp.bitwise_and(jnp.right_shift(node_id, tree_level), 1) == 1
        remaining = piece_blocks.shape[1]
        split_view = piece_blocks.reshape(row_count, remaining // 2, 2, col_width)
        lower_half = split_view[:, :, 0, :]
        upper_half = split_view[:, :, 1, :]
        kept_part = jnp.where(is_upper, upper_half, lower_half)
        sent_part = jnp.where(is_upper, lower_half, upper_half)
        received = partner(sent_part, "node", tree_level)
        first_part = jnp.where(is_upper, received, kept_part)
        second_part = jnp.where(is_upper, kept_part, received)
        totals = jnp.stack(
            [
                jnp.sum(first_part * second_part),
                jnp.sum(first_part * first_part),
                jnp.sum(second_part * second_part),
            ]
        )
        totals = lax.psum(totals, "local")
        for inner_bit in range(tree_level + 1):
            totals = totals + partner(totals, "node", inner_bit)
        piece_blocks = adasum_pair(first_part, second_part, totals[0], totals[1], totals[2])
    return piece_blocks.reshape(row_count, col_width)


def hop(value, mapping):
    z_count = lax.axis_size("node") // 2
    pairs = []
    for z in range(z_count):
        for c in range(2):
            for y in range(2):
                for x in range(2):
                    tz, tc, ty, tx = mapping(z, c, y, x)
                    pairs.append((((z * 2 + c) * 2 + y) * 2 + x, ((tz * 2 + tc) * 2 + ty) * 2 + tx))
    return lax.ppermute(value, ("node", "local"), pairs)


def split2(v):
    hi = v.astype(jnp.bfloat16)
    lo = (v - hi.astype(jnp.float32)).astype(jnp.bfloat16)
    return hi, lo


def mm(a, b):
    return jnp.dot(a, b, preferred_element_type=jnp.float32)


def low_lanes(shape):
    return lax.broadcasted_iota(jnp.int32, shape, len(shape) - 1) < HALF


def pair_pack(a, b):
    low = low_lanes(a.shape)
    axis = a.ndim - 1
    return (jnp.where(low, a, pltpu.roll(b, HALF, axis)), jnp.where(low, pltpu.roll(a, HALF, axis), b))


def lane_halves(v):
    evens, odds = [], []
    for k in range(v.shape[1] // 256):
        e, o = pair_pack(v[:, 256 * k : 256 * k + 128], v[:, 256 * k + 128 : 256 * k + 256])
        evens.append(e)
        odds.append(o)
    return jnp.concatenate(evens, axis=1), jnp.concatenate(odds, axis=1)


def split_kernel(s_ref, x_ref, own_ref, other_ref):
    even, odd = lane_halves(x_ref[...])
    up = s_ref[0] == 1
    own_ref[...] = jnp.where(up, odd, even)
    other_ref[...] = jnp.where(up, even, odd)


def residual_kernel(s_ref, x_ref, t_ref, w_ref, own_ref, other_ref, pad_ref, acc_ref):
    side = x_ref.shape[0]
    imgs, ch = x_ref.shape[2], x_ref.shape[3]
    rows = side * side * imgs
    tap = pl.program_id(0)

    @pl.when(tap == 0)
    def _():
        pad_ref[...] = jnp.zeros(pad_ref.shape, jnp.float32)
        pad_ref[1 : side + 1, 1 : side + 1] = x_ref[...]
        acc_ref[...] = -t_ref[...]

    shifted = pad_ref[pl.ds(tap // 3, side), pl.ds(tap % 3, side)].reshape(rows, ch)
    xh, xl = split2(shifted)
    wh, wl = split2(w_ref[0])
    acc_ref[...] += mm(xh, wh) + (mm(xh, wl) + mm(xl, wh))

    @pl.when(tap == pl.num_programs(0) - 1)
    def _():
        even, odd = lane_halves(acc_ref[...])
        up = s_ref[0] == 1
        own_ref[...] = jnp.where(up, odd, even)
        other_ref[...] = jnp.where(up, even, odd)


def gradient_kernel(
    scale, side, s_ref, x0, x1, x2, x3, r0, r1, r2, r3, keep_ref, send_ref, xth, xtl, rh, rl, g_ref
):
    xs, rs = (x0, x1, x2, x3), (r0, r1, r2, r3)
    rows, width = x0.shape
    strip = rows // side
    imgs = strip // side
    zero = jnp.zeros((side, 1, 4 * imgs, width), jnp.bfloat16)
    for ref in (rh, rl):
        ref[:, 0:1] = zero
        ref[:, side + 1 : side + 2] = zero
    for r in range(side):
        def gather(refs):
            parts = [ref[r * strip : (r + 1) * strip, :].reshape(side, imgs, width) for ref in refs]
            return jnp.concatenate(parts, axis=1)

        xh, xl = split2(gather(xs).reshape(4 * strip, width).T)
        xth[r] = xh
        xtl[r] = xl
        h, lo = split2(gather(rs))
        rh[r, 1 : side + 1] = h
        rl[r, 1 : side + 1] = lo

    def column(j, carry):
        for i in range(3):
            total = None
            for r in range(side):
                p = r - i + 1
                if p < 0 or p >= side:
                    continue
                bh = rh[p, pl.ds(2 - j, side)].reshape(4 * strip, width)
                bl = rl[p, pl.ds(2 - j, side)].reshape(4 * strip, width)
                part = mm(xth[r], bh) + (mm(xth[r], bl) + mm(xtl[r], bh))
                total = part if total is None else total + part
            per = width // BLK
            g_ref[pl.ds((3 * i + j) * per, per)] = (total * scale).reshape(per, BLK, width)
        return carry

    lax.fori_loop(0, 3, column, 0)
    core = s_ref[0]
    z = s_ref[1]
    half = g_ref.shape[0] // 2
    for m in range(half // 2):
        for which, out in ((core, keep_ref), (1 - core, send_ref)):
            a = g_ref[2 * m + which]
            b = g_ref[half + 2 * m + which]
            for k in range(width // 128):
                lo, hi = pair_pack(a[:, 128 * k : 128 * k + 128], b[:, 128 * k : 128 * k + 128])
                out[jnp.bitwise_xor(2 * k, z), m * BLK : (m + 1) * BLK, :] = lo
                out[jnp.bitwise_xor(2 * k + 1, z), m * BLK : (m + 1) * BLK, :] = hi


def column_sums(a, b):
    return jnp.sum((a * b).reshape(-1, a.shape[-1]), axis=0, keepdims=True)


def pair_dots_kernel(s_ref, keep_ref, received_ref, out_ref):
    core = s_ref[0]
    cross = mine = theirs = jnp.zeros((1, out_ref.shape[1]), jnp.float32)
    for d in range(keep_ref.shape[0]):
        a, b = keep_ref[d], received_ref[d]
        cross += column_sums(a, b)
        mine += column_sums(a, a)
        theirs += column_sums(b, b)
    out_ref[...] = jnp.zeros(out_ref.shape, jnp.float32)
    out_ref[0:1] = cross
    out_ref[1:2] = jnp.where(core == 0, mine, theirs)
    out_ref[2:3] = jnp.where(core == 0, theirs, mine)


def pair_coefs(cross, left_sq, right_sq):
    return 1.0 - cross / (2.0 * (left_sq + epsilon)), 1.0 - cross / (2.0 * (right_sq + epsilon))


def pair_mix_kernel(s_ref, totals_ref, keep_ref, received_ref, *out_refs):
    core = s_ref[0]
    totals = jnp.sum(totals_ref[...], axis=1, keepdims=True)
    left, right = pair_coefs(totals[0:1], totals[1:2], totals[2:3])
    keep_coef = jnp.where(core == 0, left, right)
    received_coef = jnp.where(core == 0, right, left)
    for d, out in enumerate(out_refs):
        out[...] = keep_coef * keep_ref[d] + received_coef * received_ref[d]


def gram_kernel(s_ref, s0, s1, s2, s3, gram_ref, o0, o1, o2, o3):
    core, y, z = s_ref[0], s_ref[1], s_ref[2]
    pieces = (s0, s1, s2, s3)
    for d in range(4):
        for e in range(d, 4):
            value = column_sums(pieces[d][...], pieces[e][...])
            a, b = jnp.bitwise_xor(z, d), jnp.bitwise_xor(z, e)
            gram_ref[pl.ds(4 * a + b, 1)] = value
            gram_ref[pl.ds(4 * b + a, 1)] = value
    rows = s0.shape[0] // 2
    quarter = rows // 2
    for d, piece in enumerate(pieces):
        for dx in range(2):
            start = pl.multiple_of(rows * jnp.bitwise_xor(core, dx), 8)
            first, second = pair_pack(piece[pl.ds(start, quarter)], piece[pl.ds(start + quarter, quarter)])
            (o0, o1)[dx][d] = jnp.where(y == 1, second, first)
            (o2, o3)[dx][d] = jnp.where(y == 1, first, second)


def place_kernel(s_ref, gram_ref, b0, b1, b2, b3, out_ref):
    x, y, z = s_ref[0], s_ref[1], s_ref[2]
    gram = jnp.sum(gram_ref[...], axis=1, keepdims=True)
    g = lambda a, b: gram[4 * a + b : 4 * a + b + 1]
    p = pair_coefs(g(0, 1), g(0, 0), g(1, 1)) + pair_coefs(g(2, 3), g(2, 2), g(3, 3))
    cross = p[0] * (p[2] * g(0, 2) + p[3] * g(0, 3)) + p[1] * (p[2] * g(1, 2) + p[3] * g(1, 3))
    near = p[0] * p[0] * g(0, 0) + 2.0 * p[0] * p[1] * g(0, 1) + p[1] * p[1] * g(1, 1)
    far = p[2] * p[2] * g(2, 2) + 2.0 * p[2] * p[3] * g(2, 3) + p[3] * p[3] * g(3, 3)
    near_coef, far_coef = pair_coefs(cross, near, far)
    absolute = (near_coef * p[0], near_coef * p[1], far_coef * p[2], far_coef * p[3])
    coefs = []
    for d in range(4):
        owner = jnp.bitwise_xor(z, d)
        coef = absolute[3]
        for a in range(3):
            coef = jnp.where(owner == a, absolute[a], coef)
        coefs.append(coef)
    for index, ref in enumerate((b0, b1, b2, b3)):
        dy, dx = index // 2, index % 2
        block = coefs[0] * ref[0] + coefs[1] * ref[1] + (coefs[2] * ref[2] + coefs[3] * ref[3])
        upper = pltpu.roll(block, HALF, 1)
        rows = jnp.concatenate([block[:, :HALF], upper[:, :HALF]], axis=0)
        rows = rows.reshape(out_ref.shape[0], BLK, HALF)
        slot = 2 * jnp.bitwise_xor(y, dy) + jnp.bitwise_xor(x, dx)
        for k in range(out_ref.shape[0]):
            out_ref[k, slot] = rows[k]


VM = pl.BlockSpec(memory_space=pltpu.VMEM)
SM = pl.BlockSpec(memory_space=pltpu.SMEM)


def f32(*shape):
    return jax.ShapeDtypeStruct(shape, jnp.float32)


def tile_plan(images, targets, weight):
    imgs, side, _, channels = images.shape
    width = channels // 2
    rows = side * side * imgs
    node_id = lax.axis_index("node")
    local_id = lax.axis_index("local")
    z, c = node_id // 2, node_id % 2
    y, x = local_id // 2, local_id % 2

    def scalars(*values):
        return jnp.stack([jnp.asarray(v, jnp.int32) for v in values])

    xt = jnp.transpose(images, (1, 2, 0, 3))
    x_own, x_other = pl.pallas_call(
        split_kernel,
        out_shape=(f32(rows, width), f32(rows, width)),
        in_specs=[SM, VM],
        out_specs=(VM, VM),
        name="split_images",
    )(scalars(y), xt.reshape(rows, channels))
    x_y = hop(x_other, lambda z, c, y, x: (z, c, 1 - y, x))
    x_x = hop(x_own, lambda z, c, y, x: (z, c, y, 1 - x))
    x_d = hop(x_other, lambda z, c, y, x: (z, c, 1 - y, 1 - x))

    tt = jnp.transpose(targets, (1, 2, 0, 3)).reshape(rows, channels)
    taps = weight.shape[0] * weight.shape[1]
    whole = lambda *shape: pl.BlockSpec(shape, lambda t: (0,) * len(shape))
    r_own, r_other = pl.pallas_call(
        residual_kernel,
        grid=(taps,),
        out_shape=(f32(rows, width), f32(rows, width)),
        in_specs=[
            SM,
            whole(side, side, imgs, channels),
            whole(rows, channels),
            pl.BlockSpec((1, channels, channels), lambda t: (t, 0, 0)),
        ],
        out_specs=(whole(rows, width), whole(rows, width)),
        scratch_shapes=[
            pltpu.VMEM((side + 2, side + 2, imgs, channels), jnp.float32),
            pltpu.VMEM((rows, channels), jnp.float32),
        ],
        cost_estimate=pl.CostEstimate(
            flops=6 * rows * taps * channels * channels, bytes_accessed=4 * taps * channels * channels, transcendentals=0
        ),
        name="residual",
    )(scalars(x), xt, tt, weight.reshape(taps, channels, channels))
    r_x = hop(r_other, lambda z, c, y, x: (z, c, y, 1 - x))
    r_d = hop(r_other, lambda z, c, y, x: (z, c, 1 - y, 1 - x))
    r_y = hop(r_own, lambda z, c, y, x: (z, c, 1 - y, x))

    z_count = lax.axis_size("node") // 2
    part = taps * width // 4
    keep, send = pl.pallas_call(
        lambda *refs: gradient_kernel(1.0 / rows, side, *refs),
        out_shape=(f32(z_count, part, 128), f32(z_count, part, 128)),
        in_specs=[SM] + [VM] * 8,
        out_specs=(VM, VM),
        scratch_shapes=[
            pltpu.VMEM((side, width, 4 * rows // side), jnp.bfloat16),
            pltpu.VMEM((side, width, 4 * rows // side), jnp.bfloat16),
            pltpu.VMEM((side, side + 2, 4 * imgs, width), jnp.bfloat16),
            pltpu.VMEM((side, side + 2, 4 * imgs, width), jnp.bfloat16),
            pltpu.VMEM((taps * width // BLK, BLK, width), jnp.float32),
        ],
        cost_estimate=pl.CostEstimate(
            flops=24 * rows * taps * width * width, bytes_accessed=4 * taps * width * width, transcendentals=0
        ),
        name="gradient",
    )(scalars(c, z), x_own, x_x, x_y, x_d, r_own, r_x, r_y, r_d)

    received = hop(send, lambda z, c, y, x: (z, 1 - c, y, x))
    totals = pl.pallas_call(
        pair_dots_kernel, out_shape=f32(8, 128), in_specs=[SM, VM, VM], out_specs=VM, name="pair_dots"
    )(scalars(c), keep, received)
    totals = plane_sum(totals)
    pieces = pl.pallas_call(
        pair_mix_kernel,
        out_shape=(f32(part, 128),) * z_count,
        in_specs=[SM, VM, VM, VM],
        out_specs=(VM,) * z_count,
        name="pair_mix",
    )(scalars(c), totals, keep, received)

    node = [pieces[0]]
    for d in range(1, z_count):
        node.append(hop(pieces[d], lambda z, c, y, x, d=d: (z ^ d, c, y, x)))
    gram, *blocks = pl.pallas_call(
        gram_kernel,
        out_shape=(f32(16, 128),) + (f32(z_count, part // 4, 128),) * 4,
        in_specs=[SM] + [VM] * 4,
        out_specs=(VM,) * 5,
        name="gram",
    )(scalars(c, y, z), *node)
    moved = []
    for index in range(4):
        dy, dx = index // 2, index % 2
        moved.append(hop(blocks[index], lambda z, c, y, x, dy=dy, dx=dx: (z, x, y ^ dy, c ^ dx)))
    gram = plane_sum(gram)
    for bit in (1, 2):
        gram = gram + hop(gram, lambda z, c, y, x, bit=bit: (z ^ bit, c, y, x))
    out = pl.pallas_call(
        place_kernel,
        out_shape=f32(part // 2 // BLK, 4, BLK, HALF),
        in_specs=[SM] + [VM] * 5,
        out_specs=VM,
        name="place",
    )(scalars(x, y, z), gram, *moved)
    return out.reshape(2 * part, HALF)


def plane_sum(value):
    value = value + hop(value, lambda z, c, y, x: (z, 1 - c, y, x))
    value = value + hop(value, lambda z, c, y, x: (z, c, y, 1 - x))
    return value + hop(value, lambda z, c, y, x: (z, c, 1 - y, x))


def fits(images, mesh):
    return (
        mesh.shape["local"] == 4
        and mesh.shape["node"] == 8
        and images.shape[3] == mesh.shape["node"] * HALF
        and images.shape[0] // mesh.size == 8
    )


def solution(mesh):
    def run(images, targets, weight):
        plan = tile_plan if fits(images, mesh) else general_plan
        return jax.shard_map(
            plan,
            mesh=mesh,
            in_specs=(
                P(("node", "local"), None, None, None),
                P(("node", "local"), None, None, None),
                P(),
            ),
            out_specs=P("local", "node"),
            check_vma=False,
        )(images, targets, weight)

    return run
```

```python
import jax
import jax.numpy as jnp
from jax import lax
from jax.experimental import pallas as pl
from jax.experimental.pallas import tpu as pltpu
from jax.sharding import PartitionSpec as P


epsilon = 1e-06
HALF = 64
BLK = 32


def partner(value, axis, distance):
    mask = 2**distance
    pairs = [(source, source ^ mask) for source in range(lax.axis_size(axis))]
    return lax.ppermute(value, axis, pairs)


def make_patches(images):
    side = images.shape[1]
    padded = jnp.pad(images, ((0, 0), (1, 1), (1, 1), (0, 0)))
    tap_views = []
    for row_shift in range(3):
        for col_shift in range(3):
            tap_views.append(padded[:, row_shift : row_shift + side, col_shift : col_shift + side, :])
    joined = jnp.concatenate(tap_views, axis=-1)
    return joined.reshape(-1, 9 * images.shape[3])


def adasum_pair(left_vec, right_vec, cross_sum, left_sq, right_sq):
    left_coef = 1.0 - cross_sum / (2.0 * (left_sq + epsilon))
    right_coef = 1.0 - cross_sum / (2.0 * (right_sq + epsilon))
    return left_coef * left_vec + right_coef * right_vec


def general_plan(images, targets, weight):
    channels = images.shape[3]
    flat_w = weight.reshape(9 * channels, channels)
    patches = make_patches(images)
    outputs = jnp.dot(patches, flat_w, precision=lax.Precision.HIGHEST, preferred_element_type=jnp.float32)
    residual = outputs - targets.reshape(-1, channels)
    row_scale = 1.0 / patches.shape[0]
    product = lax.dot_general(
        patches,
        residual,
        (((0,), (0,)), ((), ())),
        precision=lax.Precision.HIGHEST,
        preferred_element_type=jnp.float32,
    )
    my_rows = lax.psum_scatter(product * row_scale, "local", scatter_dimension=0, tiled=True)
    node_count = lax.axis_size("node")
    levels = node_count.bit_length() - 1
    row_count = my_rows.shape[0]
    col_width = channels // node_count
    node_id = lax.axis_index("node")
    piece_blocks = my_rows.reshape(row_count, node_count, col_width)
    for tree_level in range(levels):
        is_upper = jnp.bitwise_and(jnp.right_shift(node_id, tree_level), 1) == 1
        remaining = piece_blocks.shape[1]
        split_view = piece_blocks.reshape(row_count, remaining // 2, 2, col_width)
        lower_half = split_view[:, :, 0, :]
        upper_half = split_view[:, :, 1, :]
        kept_part = jnp.where(is_upper, upper_half, lower_half)
        sent_part = jnp.where(is_upper, lower_half, upper_half)
        received = partner(sent_part, "node", tree_level)
        first_part = jnp.where(is_upper, received, kept_part)
        second_part = jnp.where(is_upper, kept_part, received)
        totals = jnp.stack(
            [
                jnp.sum(first_part * second_part),
                jnp.sum(first_part * first_part),
                jnp.sum(second_part * second_part),
            ]
        )
        totals = lax.psum(totals, "local")
        for inner_bit in range(tree_level + 1):
            totals = totals + partner(totals, "node", inner_bit)
        piece_blocks = adasum_pair(first_part, second_part, totals[0], totals[1], totals[2])
    return piece_blocks.reshape(row_count, col_width)


def hop(value, mapping):
    z_count = lax.axis_size("node") // 2
    pairs = []
    for z in range(z_count):
        for c in range(2):
            for y in range(2):
                for x in range(2):
                    tz, tc, ty, tx = mapping(z, c, y, x)
                    pairs.append((((z * 2 + c) * 2 + y) * 2 + x, ((tz * 2 + tc) * 2 + ty) * 2 + tx))
    return lax.ppermute(value, ("node", "local"), pairs)


def split2(v):
    hi = v.astype(jnp.bfloat16)
    lo = (v - hi.astype(jnp.float32)).astype(jnp.bfloat16)
    return hi, lo


def mm(a, b):
    return jnp.dot(a, b, preferred_element_type=jnp.float32)


def low_lanes(shape):
    return lax.broadcasted_iota(jnp.int32, shape, len(shape) - 1) < HALF


def pair_pack(a, b):
    low = low_lanes(a.shape)
    axis = a.ndim - 1
    return (jnp.where(low, a, pltpu.roll(b, HALF, axis)), jnp.where(low, pltpu.roll(a, HALF, axis), b))


def lane_halves(v):
    evens, odds = [], []
    for k in range(v.shape[1] // 256):
        e, o = pair_pack(v[:, 256 * k : 256 * k + 128], v[:, 256 * k + 128 : 256 * k + 256])
        evens.append(e)
        odds.append(o)
    return jnp.concatenate(evens, axis=1), jnp.concatenate(odds, axis=1)


def split_kernel(s_ref, x_ref, own_ref, other_ref):
    even, odd = lane_halves(x_ref[...])
    up = s_ref[0] == 1
    own_ref[...] = jnp.where(up, odd, even)
    other_ref[...] = jnp.where(up, even, odd)


def residual_kernel(s_ref, x_ref, t_ref, w_ref, own_ref, other_ref, pad_ref, acc_ref):
    side = x_ref.shape[0]
    imgs, ch = x_ref.shape[2], x_ref.shape[3]
    rows = side * side * imgs
    tap = pl.program_id(0)

    @pl.when(tap == 0)
    def _():
        pad_ref[...] = jnp.zeros(pad_ref.shape, jnp.float32)
        pad_ref[1 : side + 1, 1 : side + 1] = x_ref[...]
        acc_ref[...] = -t_ref[...]

    shifted = pad_ref[pl.ds(tap // 3, side), pl.ds(tap % 3, side)].reshape(rows, ch)
    xh, xl = split2(shifted)
    wh, wl = split2(w_ref[0])
    acc_ref[...] += mm(xh, wh) + (mm(xh, wl) + mm(xl, wh))

    @pl.when(tap == pl.num_programs(0) - 1)
    def _():
        even, odd = lane_halves(acc_ref[...])
        up = s_ref[0] == 1
        own_ref[...] = jnp.where(up, odd, even)
        other_ref[...] = jnp.where(up, even, odd)


def gradient_kernel(
    scale, side, s_ref, x0, x1, x2, x3, r0, r1, r2, r3, keep_ref, send_ref, xt, rh, rl, g_ref
):
    xs, rs = (x0, x1, x2, x3), (r0, r1, r2, r3)
    rows, width = x0.shape
    strip = rows // side
    imgs = strip // side
    span = (side + 1) * 4 * imgs
    for ref in (rh, rl):
        for edge in (0, side + 1, side + 2):
            ref[:, edge] = jnp.zeros((side, 4 * imgs, width), jnp.bfloat16)
    for r in range(side):
        def gather(refs):
            parts = [ref[r * strip : (r + 1) * strip, :].reshape(side, imgs, width) for ref in refs]
            return jnp.concatenate(parts, axis=1)

        rows_x = gather(xs).reshape(4 * strip, width)
        rows_x = jnp.concatenate([rows_x, jnp.zeros((span - 4 * strip, width), jnp.float32)], axis=0)
        xh, xl = split2(rows_x.T)
        xt[r, :, 0:span] = xh
        xt[r, :, span : 2 * span] = xh
        xt[r, :, 2 * span : 3 * span] = xl
        h, lo = split2(gather(rs))
        rh[r, 1 : side + 1] = h
        rl[r, 1 : side + 1] = lo

    def column(j, carry):
        for i in range(3):
            total = None
            for r in range(side):
                p = r - i + 1
                if p < 0 or p >= side:
                    continue
                bh = rh[p, pl.ds(2 - j, side + 1)].reshape(span, width)
                bl = rl[p, pl.ds(2 - j, side + 1)].reshape(span, width)
                part = mm(xt[r], jnp.concatenate([bh, bl, bh], axis=0))
                total = part if total is None else total + part
            per = width // BLK
            g_ref[pl.ds((3 * i + j) * per, per)] = (total * scale).reshape(per, BLK, width)
        return carry

    lax.fori_loop(0, 3, column, 0)
    odd = s_ref[0] == 1
    per = g_ref.shape[0] // 8
    for quarter in range(4):
        for k in range(width // 128):
            slot = 4 * jnp.bitwise_xor(k, s_ref[1]) + 2 * jnp.bitwise_xor(quarter // 2, s_ref[2])
            slot = slot + jnp.bitwise_xor(quarter % 2, s_ref[3])
            for m in range(per):
                a = g_ref[2 * per * quarter + m, :, 128 * k : 128 * k + 128]
                b = g_ref[2 * per * quarter + per + m, :, 128 * k : 128 * k + 128]
                first, second = pair_pack(a, b)
                keep_ref[slot, m * BLK : (m + 1) * BLK, :] = jnp.where(odd, second, first)
                send_ref[slot, m * BLK : (m + 1) * BLK, :] = jnp.where(odd, first, second)


def column_sums(a, b):
    return jnp.sum((a * b).reshape(-1, a.shape[-1]), axis=0, keepdims=True)


def fetch(sources, slots, sems):
    copies = [pltpu.make_async_copy(src, dst, sems.at[i]) for i, (src, dst) in enumerate(zip(sources, slots))]
    for copy in copies:
        copy.start()
    return copies


def pair_dots_kernel(s_ref, keep_ref, received_ref, out_ref, buf, sems):
    core = s_ref[0]
    count = keep_ref.shape[0]
    sources = [ref.at[d] for d in range(count) for ref in (keep_ref, received_ref)]
    copies = fetch(sources, [buf.at[i] for i in range(2 * count)], sems)
    cross = mine = theirs = jnp.zeros((1, out_ref.shape[1]), jnp.float32)
    for d in range(count):
        copies[2 * d].wait()
        copies[2 * d + 1].wait()
        a, b = buf[2 * d], buf[2 * d + 1]
        cross += column_sums(a, b)
        mine += column_sums(a, a)
        theirs += column_sums(b, b)
    out_ref[...] = jnp.zeros(out_ref.shape, jnp.float32)
    out_ref[0:1] = cross
    out_ref[1:2] = jnp.where(core == 0, mine, theirs)
    out_ref[2:3] = jnp.where(core == 0, theirs, mine)


def pair_coefs(cross, left_sq, right_sq):
    return 1.0 - cross / (2.0 * (left_sq + epsilon)), 1.0 - cross / (2.0 * (right_sq + epsilon))


def pair_mix_kernel(s_ref, totals_ref, keep_ref, received_ref, *refs):
    core = s_ref[0]
    count = keep_ref.shape[0]
    out_refs, (buf, in_sems, out_sems) = refs[:count], refs[count:]
    order = list(range(count - 1, -1, -1))
    sources = [ref.at[d] for d in order for ref in (keep_ref, received_ref)]
    copies = fetch(sources, [buf.at[i] for i in range(2 * count)], in_sems)
    totals = jnp.sum(totals_ref[...], axis=1, keepdims=True)
    left, right = pair_coefs(totals[0:1], totals[1:2], totals[2:3])
    keep_coef = jnp.where(core == 0, left, right)
    received_coef = jnp.where(core == 0, right, left)
    stores = []
    for i, d in enumerate(order):
        copies[2 * i].wait()
        copies[2 * i + 1].wait()
        buf[2 * i] = keep_coef * buf[2 * i] + received_coef * buf[2 * i + 1]
        stores.append(pltpu.make_async_copy(buf.at[2 * i], out_refs[d], out_sems.at[i]))
        stores[-1].start()
    for store in stores:
        store.wait()


def gram_kernel(s_ref, *refs):
    upper, x = s_ref[0], s_ref[1]
    blocks, (gram_ref, buf, sems) = refs[:8], refs[8:]
    copies = fetch(blocks, [buf.at[slot_of(i)] for i in range(8)], sems)
    node = [2 * jnp.bitwise_xor(upper, d // 2) + jnp.bitwise_xor(x, d % 2) for d in range(4)]
    for i in (0, 1, 2, 3, 4, 5, 6, 7):
        copies[i].wait()
    for e in range(4):
        for d in range(e + 1):
            value = column_sums(buf[2 * d : 2 * d + 2], buf[2 * e : 2 * e + 2])
            gram_ref[pl.ds(4 * node[d] + node[e], 1)] = value
            gram_ref[pl.ds(4 * node[e] + node[d], 1)] = value


def slot_of(index):
    e, dy, dx = index // 4, index // 2 % 2, index % 2
    return 4 * e + 2 * dx + dy


def place_kernel(s_ref, gram_ref, *refs):
    upper, x, y = s_ref[0], s_ref[1], s_ref[2]
    blocks, (out_ref, parts, rows_ref, sems) = refs[:8], refs[8:]
    copies = fetch(blocks, [parts.at[slot_of(i)] for i in range(8)], sems)
    gram = jnp.sum(gram_ref[...], axis=1, keepdims=True)
    g = lambda a, b: gram[4 * a + b : 4 * a + b + 1]
    p = pair_coefs(g(0, 1), g(0, 0), g(1, 1)) + pair_coefs(g(2, 3), g(2, 2), g(3, 3))
    cross = p[0] * (p[2] * g(0, 2) + p[3] * g(0, 3)) + p[1] * (p[2] * g(1, 2) + p[3] * g(1, 3))
    near = p[0] * p[0] * g(0, 0) + 2.0 * p[0] * p[1] * g(0, 1) + p[1] * p[1] * g(1, 1)
    far = p[2] * p[2] * g(2, 2) + 2.0 * p[2] * p[3] * g(2, 3) + p[3] * p[3] * g(3, 3)
    near_coef, far_coef = pair_coefs(cross, near, far)
    absolute = (near_coef * p[0], near_coef * p[1], far_coef * p[2], far_coef * p[3])
    coefs = []
    for d in range(4):
        owner = 2 * jnp.bitwise_xor(upper, d // 2) + jnp.bitwise_xor(x, d % 2)
        coef = absolute[3]
        for a in range(3):
            coef = jnp.where(owner == a, absolute[a], coef)
        coefs.append(coef)
    for copy in copies:
        copy.wait()
    for dy in range(2):
        part = [parts[2 * d + dy] for d in range(4)]
        block = coefs[0] * part[0] + coefs[1] * part[1] + (coefs[2] * part[2] + coefs[3] * part[3])
        upper_half = pltpu.roll(block, HALF, 1)
        rows = jnp.concatenate([block[:, :HALF], upper_half[:, :HALF]], axis=0)
        rows = rows.reshape(rows_ref.shape[0], HALF, HALF)
        slot = jnp.bitwise_xor(y, dy)
        for k in range(rows_ref.shape[0]):
            rows_ref[k, slot] = rows[k]
    out_ref[...] = rows_ref[...].reshape(out_ref.shape[1], HALF).T


VM = pl.BlockSpec(memory_space=pltpu.VMEM)
HB = pl.BlockSpec(memory_space=pltpu.HBM)
SM = pl.BlockSpec(memory_space=pltpu.SMEM)


def f32(*shape):
    return jax.ShapeDtypeStruct(shape, jnp.float32)


def tile_plan(images, targets, weight):
    return tiles(images, targets, weight)


def tiles(images, targets, weight):
    imgs, side, _, channels = images.shape
    width = channels // 2
    rows = side * side * imgs
    node_id = lax.axis_index("node")
    local_id = lax.axis_index("local")
    z, c = node_id // 2, node_id % 2
    y, x = local_id // 2, local_id % 2

    def scalars(*values):
        return jnp.stack([jnp.asarray(v, jnp.int32) for v in values])

    xt = jnp.transpose(images, (1, 2, 0, 3))
    x_own, x_other = pl.pallas_call(
        split_kernel,
        out_shape=(f32(rows, width), f32(rows, width)),
        in_specs=[SM, VM],
        out_specs=(VM, VM),
        name="split_images",
    )(scalars(y), xt.reshape(rows, channels))
    x_y = hop(x_other, lambda z, c, y, x: (z, c, 1 - y, x))
    x_x = hop(x_own, lambda z, c, y, x: (z, c, y, 1 - x))
    x_d = hop(x_other, lambda z, c, y, x: (z, c, 1 - y, 1 - x))

    tt = jnp.transpose(targets, (1, 2, 0, 3)).reshape(rows, channels)
    taps = weight.shape[0] * weight.shape[1]
    whole = lambda *shape: pl.BlockSpec(shape, lambda t: (0,) * len(shape))
    r_own, r_other = pl.pallas_call(
        residual_kernel,
        grid=(taps,),
        out_shape=(f32(rows, width), f32(rows, width)),
        in_specs=[
            SM,
            whole(side, side, imgs, channels),
            whole(rows, channels),
            pl.BlockSpec((1, channels, channels), lambda t: (t, 0, 0)),
        ],
        out_specs=(whole(rows, width), whole(rows, width)),
        scratch_shapes=[
            pltpu.VMEM((side + 2, side + 2, imgs, channels), jnp.float32),
            pltpu.VMEM((rows, channels), jnp.float32),
        ],
        cost_estimate=pl.CostEstimate(
            flops=6 * rows * taps * channels * channels, bytes_accessed=4 * taps * channels * channels, transcendentals=0
        ),
        name="residual",
    )(scalars(x), xt, tt, weight.reshape(taps, channels, channels))
    r_x = hop(r_other, lambda z, c, y, x: (z, c, y, 1 - x))
    r_d = hop(r_other, lambda z, c, y, x: (z, c, 1 - y, 1 - x))
    r_y = hop(r_own, lambda z, c, y, x: (z, c, 1 - y, x))

    z_count = lax.axis_size("node") // 2
    part = taps * width // 8
    count = 2 * z_count
    place = scalars(z // 2, x, y)
    keep, send = pl.pallas_call(
        lambda *refs: gradient_kernel(1.0 / rows, side, *refs),
        out_shape=(f32(count, part, 128), f32(count, part, 128)),
        in_specs=[SM] + [VM] * 8,
        out_specs=(VM, VM),
        scratch_shapes=[
            pltpu.VMEM((side, width, 3 * (side + 1) * 4 * imgs), jnp.bfloat16),
            pltpu.VMEM((side, side + 3, 4 * imgs, width), jnp.bfloat16),
            pltpu.VMEM((side, side + 3, 4 * imgs, width), jnp.bfloat16),
            pltpu.VMEM((taps * width // BLK, BLK, width), jnp.float32),
        ],
        cost_estimate=pl.CostEstimate(
            flops=24 * rows * taps * width * width, bytes_accessed=4 * taps * width * width, transcendentals=0
        ),
        name="gradient",
    )(scalars(c, z // 2, y, z % 2), x_own, x_x, x_y, x_d, r_own, r_x, r_y, r_d)

    received = hop(send, lambda z, c, y, x: (z, 1 - c, y, x))
    totals = pl.pallas_call(
        pair_dots_kernel,
        out_shape=f32(8, 128),
        in_specs=[SM, HB, HB],
        out_specs=VM,
        scratch_shapes=[pltpu.VMEM((2 * count, part, 128), jnp.float32), pltpu.SemaphoreType.DMA((2 * count,))],
        name="pair_dots",
    )(scalars(c), keep, received)
    totals = plane_sum(totals)
    blocks = pl.pallas_call(
        pair_mix_kernel,
        out_shape=(f32(part, 128),) * count,
        in_specs=[SM, VM, HB, HB],
        out_specs=(HB,) * count,
        scratch_shapes=[
            pltpu.VMEM((2 * count, part, 128), jnp.float32),
            pltpu.SemaphoreType.DMA((2 * count,)),
            pltpu.SemaphoreType.DMA((count,)),
        ],
        name="pair_mix",
    )(scalars(c), totals, keep, received)

    moved = []
    for index in range(count):
        e, dy, dx = index // 4, index // 2 % 2, index % 2
        mapping = lambda z, c, y, x, e=e, dy=dy, dx=dx: (2 * (z // 2 ^ e) + c, x, y ^ dy, z % 2 ^ dx)
        moved.append(hop(blocks[index], mapping))
    gram = pl.pallas_call(
        gram_kernel,
        out_shape=f32(16, 128),
        in_specs=[SM] + [HB] * count,
        out_specs=VM,
        scratch_shapes=[pltpu.VMEM((count, part, 128), jnp.float32), pltpu.SemaphoreType.DMA((count,))],
        name="gram",
    )(place, *moved)
    along = [hop(gram, lambda z, c, y, x, d=d: (z ^ d, c, y, x)) for d in range(1, z_count)]
    gram = plane_sum((gram + along[0]) + (along[1] + along[2]))
    out = pl.pallas_call(
        place_kernel,
        out_shape=f32(HALF, 4 * part),
        in_specs=[SM, VM] + [HB] * count,
        out_specs=VM,
        scratch_shapes=[
            pltpu.VMEM((count, part, 128), jnp.float32),
            pltpu.VMEM((2 * part // HALF, 2, HALF, HALF), jnp.float32),
            pltpu.SemaphoreType.DMA((count,)),
        ],
        name="place",
    )(place, gram, *moved)
    return out.T


def plane_sum(value):
    value = value + hop(value, lambda z, c, y, x: (z, 1 - c, y, x))
    across = [hop(value, lambda z, c, y, x, d=d: (z, c, y ^ (d >> 1), x ^ (d & 1))) for d in (1, 2, 3)]
    return (value + across[0]) + (across[1] + across[2])


def fits(images, mesh):
    return (
        mesh.shape["local"] == 4
        and mesh.shape["node"] == 8
        and images.shape[3] == mesh.shape["node"] * HALF
        and images.shape[0] // mesh.size == 8
    )


def solution(mesh):
    def run(images, targets, weight):
        tiled = fits(images, mesh)
        step = jax.shard_map(
            tile_plan if tiled else general_plan,
            mesh=mesh,
            in_specs=(
                P(("node", "local"), None, None, None),
                P(("node", "local"), None, None, None),
                P(),
            ),
            out_specs=P("local", "node"),
            check_vma=False,
        )
        return step(images, targets, weight)

    return run
```

```python
import jax
import jax.numpy as jnp
from jax import lax
from jax.experimental import pallas as pl
from jax.experimental.pallas import tpu as pltpu
from jax.sharding import PartitionSpec as P


epsilon = 1e-06
HALF = 64
BLK = 32
FULL = 65 * 2**20


def partner(value, axis, distance):
    mask = 2**distance
    pairs = [(source, source ^ mask) for source in range(lax.axis_size(axis))]
    return lax.ppermute(value, axis, pairs)


def make_patches(images):
    side = images.shape[1]
    padded = jnp.pad(images, ((0, 0), (1, 1), (1, 1), (0, 0)))
    tap_views = []
    for row_shift in range(3):
        for col_shift in range(3):
            tap_views.append(padded[:, row_shift : row_shift + side, col_shift : col_shift + side, :])
    joined = jnp.concatenate(tap_views, axis=-1)
    return joined.reshape(-1, 9 * images.shape[3])


def adasum_pair(left_vec, right_vec, cross_sum, left_sq, right_sq):
    left_coef = 1.0 - cross_sum / (2.0 * (left_sq + epsilon))
    right_coef = 1.0 - cross_sum / (2.0 * (right_sq + epsilon))
    return left_coef * left_vec + right_coef * right_vec


def general_plan(images, targets, weight):
    channels = images.shape[3]
    flat_w = weight.reshape(9 * channels, channels)
    patches = make_patches(images)
    outputs = jnp.dot(patches, flat_w, precision=lax.Precision.HIGHEST, preferred_element_type=jnp.float32)
    residual = outputs - targets.reshape(-1, channels)
    row_scale = 1.0 / patches.shape[0]
    product = lax.dot_general(
        patches,
        residual,
        (((0,), (0,)), ((), ())),
        precision=lax.Precision.HIGHEST,
        preferred_element_type=jnp.float32,
    )
    my_rows = lax.psum_scatter(product * row_scale, "local", scatter_dimension=0, tiled=True)
    node_count = lax.axis_size("node")
    levels = node_count.bit_length() - 1
    row_count = my_rows.shape[0]
    col_width = channels // node_count
    node_id = lax.axis_index("node")
    piece_blocks = my_rows.reshape(row_count, node_count, col_width)
    for tree_level in range(levels):
        is_upper = jnp.bitwise_and(jnp.right_shift(node_id, tree_level), 1) == 1
        remaining = piece_blocks.shape[1]
        split_view = piece_blocks.reshape(row_count, remaining // 2, 2, col_width)
        lower_half = split_view[:, :, 0, :]
        upper_half = split_view[:, :, 1, :]
        kept_part = jnp.where(is_upper, upper_half, lower_half)
        sent_part = jnp.where(is_upper, lower_half, upper_half)
        received = partner(sent_part, "node", tree_level)
        first_part = jnp.where(is_upper, received, kept_part)
        second_part = jnp.where(is_upper, kept_part, received)
        totals = jnp.stack(
            [
                jnp.sum(first_part * second_part),
                jnp.sum(first_part * first_part),
                jnp.sum(second_part * second_part),
            ]
        )
        totals = lax.psum(totals, "local")
        for inner_bit in range(tree_level + 1):
            totals = totals + partner(totals, "node", inner_bit)
        piece_blocks = adasum_pair(first_part, second_part, totals[0], totals[1], totals[2])
    return piece_blocks.reshape(row_count, col_width)


def hop(value, mapping):
    z_count = lax.axis_size("node") // 2
    pairs = []
    for z in range(z_count):
        for c in range(2):
            for y in range(2):
                for x in range(2):
                    tz, tc, ty, tx = mapping(z, c, y, x)
                    pairs.append((((z * 2 + c) * 2 + y) * 2 + x, ((tz * 2 + tc) * 2 + ty) * 2 + tx))
    return lax.ppermute(value, ("node", "local"), pairs)


def split2(v):
    hi = v.astype(jnp.bfloat16)
    lo = (v - hi.astype(jnp.float32)).astype(jnp.bfloat16)
    return hi, lo


def mm(a, b):
    return jnp.dot(a, b, preferred_element_type=jnp.float32)


def low_lanes(shape):
    return lax.broadcasted_iota(jnp.int32, shape, len(shape) - 1) < HALF


def pair_pack(a, b):
    low = low_lanes(a.shape)
    axis = a.ndim - 1
    return (jnp.where(low, a, pltpu.roll(b, HALF, axis)), jnp.where(low, pltpu.roll(a, HALF, axis), b))


def lane_halves(v):
    evens, odds = [], []
    for k in range(v.shape[1] // 256):
        e, o = pair_pack(v[:, 256 * k : 256 * k + 128], v[:, 256 * k + 128 : 256 * k + 256])
        evens.append(e)
        odds.append(o)
    return jnp.concatenate(evens, axis=1), jnp.concatenate(odds, axis=1)


def split_kernel(s_ref, x_ref, own_ref, other_ref, buf, halves, in_sems, out_sems):
    strips, strip, _ = buf.shape
    spans = [pl.ds(r * strip, strip) for r in range(strips)]
    copies = fetch([x_ref.at[span] for span in spans], [buf.at[r] for r in range(strips)], in_sems)
    up = s_ref[0] == 1
    stores = []
    for r in range(strips):
        copies[r].wait()
        even, odd = lane_halves(buf[r])
        halves[2 * r] = jnp.where(up, odd, even)
        halves[2 * r + 1] = jnp.where(up, even, odd)
        for k, ref in enumerate((own_ref, other_ref)):
            stores.append(pltpu.make_async_copy(halves.at[2 * r + k], ref.at[spans[r]], out_sems.at[2 * r + k]))
            stores[-1].start()
    for store in stores:
        store.wait()


def residual_kernel(s_ref, x_ref, t_ref, w_ref, own_ref, other_ref, pad_ref, acc_ref):
    side = x_ref.shape[0]
    imgs, ch = x_ref.shape[2], x_ref.shape[3]
    rows = side * side * imgs
    tap = pl.program_id(0)

    @pl.when(tap == 0)
    def _():
        pad_ref[...] = jnp.zeros(pad_ref.shape, jnp.float32)
        pad_ref[1 : side + 1, 1 : side + 1] = x_ref[...]
        acc_ref[...] = -t_ref[...]

    shifted = pad_ref[pl.ds(tap // 3, side), pl.ds(tap % 3, side)].reshape(rows, ch)
    xh, xl = split2(shifted)
    wh, wl = split2(w_ref[0])
    acc_ref[...] += mm(xh, wh) + (mm(xh, wl) + mm(xl, wh))

    @pl.when(tap == pl.num_programs(0) - 1)
    def _():
        even, odd = lane_halves(acc_ref[...])
        up = s_ref[0] == 1
        own_ref[...] = jnp.where(up, odd, even)
        other_ref[...] = jnp.where(up, even, odd)


def gradient_kernel(scale, side, s_ref, *refs):
    sources, (keep_ref, send_ref, buf, xt, rh, rl, g_ref, sems) = refs[:8], refs[8:]
    copies = fetch(sources, [buf.at[i] for i in range(8)], sems)
    _, rows, width = buf.shape
    strip = rows // side
    imgs = strip // side
    span = (side + 1) * 4 * imgs
    for ref in (rh, rl):
        for edge in (0, side + 1, side + 2):
            ref[:, edge] = jnp.zeros((side, 4 * imgs, width), jnp.bfloat16)

    def gather(base, r):
        parts = [buf[base + i, r * strip : (r + 1) * strip, :].reshape(side, imgs, width) for i in range(4)]
        return jnp.concatenate(parts, axis=1)

    for copy in copies[:4]:
        copy.wait()
    for r in range(side):
        rows_x = gather(0, r).reshape(4 * strip, width)
        rows_x = jnp.concatenate([rows_x, jnp.zeros((span - 4 * strip, width), jnp.float32)], axis=0)
        xh, xl = split2(rows_x.T)
        xt[r, :, 0:span] = xh
        xt[r, :, span : 2 * span] = xh
        xt[r, :, 2 * span : 3 * span] = xl
    for copy in copies[4:]:
        copy.wait()
    for r in range(side):
        h, lo = split2(gather(4, r))
        rh[r, 1 : side + 1] = h
        rl[r, 1 : side + 1] = lo

    def column(j, carry):
        totals = [None] * 3
        for p in range(side):
            first, last = max(p - 1, 0), min(p + 1, side - 1)
            bh = rh[p, pl.ds(2 - j, side + 1)].reshape(span, width)
            bl = rl[p, pl.ds(2 - j, side + 1)].reshape(span, width)
            left = xt[first : last + 1].reshape((last + 1 - first) * width, 3 * span)
            product = mm(left, jnp.concatenate([bh, bl, bh], axis=0))
            for r in range(first, last + 1):
                i = r - p + 1
                part = product[(r - first) * width : (r - first + 1) * width]
                totals[i] = part if totals[i] is None else totals[i] + part
        per = width // BLK
        for i in range(3):
            g_ref[pl.ds((3 * i + j) * per, per)] = (totals[i] * scale).reshape(per, BLK, width)
        return carry

    lax.fori_loop(0, 3, column, 0)
    odd = s_ref[0] == 1
    per = g_ref.shape[0] // 8
    for quarter in range(4):
        for k in range(width // 128):
            slot = 4 * jnp.bitwise_xor(k, s_ref[1]) + 2 * jnp.bitwise_xor(quarter // 2, s_ref[2])
            slot = slot + jnp.bitwise_xor(quarter % 2, s_ref[3])
            for m in range(per):
                a = g_ref[2 * per * quarter + m, :, 128 * k : 128 * k + 128]
                b = g_ref[2 * per * quarter + per + m, :, 128 * k : 128 * k + 128]
                first, second = pair_pack(a, b)
                keep_ref[slot, m * BLK : (m + 1) * BLK, :] = jnp.where(odd, second, first)
                send_ref[slot, m * BLK : (m + 1) * BLK, :] = jnp.where(odd, first, second)


def column_sums(a, b):
    return jnp.sum((a * b).reshape(-1, a.shape[-1]), axis=0, keepdims=True)


def fetch(sources, slots, sems):
    copies = [pltpu.make_async_copy(src, dst, sems.at[i]) for i, (src, dst) in enumerate(zip(sources, slots))]
    for copy in copies:
        copy.start()
    return copies


def pair_dots_kernel(s_ref, keep_ref, received_ref, out_ref, buf, sems):
    core = s_ref[0]
    count = keep_ref.shape[0]
    sources = [ref.at[d] for d in range(count) for ref in (keep_ref, received_ref)]
    copies = fetch(sources, [buf.at[i] for i in range(2 * count)], sems)
    cross = mine = theirs = jnp.zeros((1, out_ref.shape[1]), jnp.float32)
    for d in range(count):
        copies[2 * d].wait()
        copies[2 * d + 1].wait()
        a, b = buf[2 * d], buf[2 * d + 1]
        cross += column_sums(a, b)
        mine += column_sums(a, a)
        theirs += column_sums(b, b)
    out_ref[...] = jnp.zeros(out_ref.shape, jnp.float32)
    out_ref[0:1] = cross
    out_ref[1:2] = jnp.where(core == 0, mine, theirs)
    out_ref[2:3] = jnp.where(core == 0, theirs, mine)


def sum_four(refs):
    return (refs[0][...] + refs[1][...]) + (refs[2][...] + refs[3][...])


def pair_coefs(cross, left_sq, right_sq):
    return 1.0 - cross / (2.0 * (left_sq + epsilon)), 1.0 - cross / (2.0 * (right_sq + epsilon))


def pair_mix_kernel(s_ref, t0, t1, t2, t3, keep_ref, received_ref, *refs):
    totals_refs = (t0, t1, t2, t3)
    core = s_ref[0]
    count = keep_ref.shape[0]
    out_refs, (buf, in_sems, out_sems) = refs[:count], refs[count:]
    order = list(range(count - 1, -1, -1))
    sources = [ref.at[d] for d in order for ref in (keep_ref, received_ref)]
    copies = fetch(sources, [buf.at[i] for i in range(2 * count)], in_sems)
    totals = jnp.sum(sum_four(totals_refs), axis=1, keepdims=True)
    left, right = pair_coefs(totals[0:1], totals[1:2], totals[2:3])
    keep_coef = jnp.where(core == 0, left, right)
    received_coef = jnp.where(core == 0, right, left)
    stores = []
    for i, d in enumerate(order):
        copies[2 * i].wait()
        copies[2 * i + 1].wait()
        buf[2 * i] = keep_coef * buf[2 * i] + received_coef * buf[2 * i + 1]
        stores.append(pltpu.make_async_copy(buf.at[2 * i], out_refs[d], out_sems.at[i]))
        stores[-1].start()
    for store in stores:
        store.wait()


def gram_kernel(s_ref, *refs):
    upper, x = s_ref[0], s_ref[1]
    blocks, (gram_ref, buf, sems) = refs[:8], refs[8:]
    copies = fetch(blocks, [buf.at[slot_of(i)] for i in range(8)], sems)
    node = [2 * jnp.bitwise_xor(upper, d // 2) + jnp.bitwise_xor(x, d % 2) for d in range(4)]
    for i in (0, 1, 2, 3, 4, 5, 6, 7):
        copies[i].wait()
    for e in range(4):
        for d in range(e + 1):
            value = column_sums(buf[2 * d : 2 * d + 2], buf[2 * e : 2 * e + 2])
            gram_ref[pl.ds(4 * node[d] + node[e], 1)] = value
            gram_ref[pl.ds(4 * node[e] + node[d], 1)] = value


def slot_of(index):
    e, dy, dx = index // 4, index // 2 % 2, index % 2
    return 4 * e + 2 * dx + dy


def place_kernel(s_ref, g0, g1, g2, g3, *refs):
    upper, x, y = s_ref[0], s_ref[1], s_ref[2]
    blocks, (out_ref, parts, rows_ref, sems) = refs[:8], refs[8:]
    copies = fetch(blocks, [parts.at[slot_of(i)] for i in range(8)], sems)
    gram = jnp.sum(sum_four((g0, g1, g2, g3)), axis=1, keepdims=True)
    g = lambda a, b: gram[4 * a + b : 4 * a + b + 1]
    p = pair_coefs(g(0, 1), g(0, 0), g(1, 1)) + pair_coefs(g(2, 3), g(2, 2), g(3, 3))
    cross = p[0] * (p[2] * g(0, 2) + p[3] * g(0, 3)) + p[1] * (p[2] * g(1, 2) + p[3] * g(1, 3))
    near = p[0] * p[0] * g(0, 0) + 2.0 * p[0] * p[1] * g(0, 1) + p[1] * p[1] * g(1, 1)
    far = p[2] * p[2] * g(2, 2) + 2.0 * p[2] * p[3] * g(2, 3) + p[3] * p[3] * g(3, 3)
    near_coef, far_coef = pair_coefs(cross, near, far)
    absolute = (near_coef * p[0], near_coef * p[1], far_coef * p[2], far_coef * p[3])
    coefs = []
    for d in range(4):
        owner = 2 * jnp.bitwise_xor(upper, d // 2) + jnp.bitwise_xor(x, d % 2)
        coef = absolute[3]
        for a in range(3):
            coef = jnp.where(owner == a, absolute[a], coef)
        coefs.append(coef)
    for copy in copies:
        copy.wait()
    for dy in range(2):
        part = [parts[2 * d + dy] for d in range(4)]
        block = coefs[0] * part[0] + coefs[1] * part[1] + (coefs[2] * part[2] + coefs[3] * part[3])
        upper_half = pltpu.roll(block, HALF, 1)
        rows = jnp.concatenate([block[:, :HALF], upper_half[:, :HALF]], axis=0)
        rows = rows.reshape(rows_ref.shape[0], HALF, HALF)
        slot = jnp.bitwise_xor(y, dy)
        for k in range(rows_ref.shape[0]):
            rows_ref[k, slot] = rows[k]
    out_ref[...] = rows_ref[...].reshape(out_ref.shape[1], HALF).T


VM = pl.BlockSpec(memory_space=pltpu.VMEM)
HB = pl.BlockSpec(memory_space=pltpu.HBM)
SM = pl.BlockSpec(memory_space=pltpu.SMEM)


def f32(*shape):
    return jax.ShapeDtypeStruct(shape, jnp.float32)


def tile_plan(images, targets, weight):
    return tiles(images, targets, weight)


def tiles(images, targets, weight):
    imgs, side, _, channels = images.shape
    width = channels // 2
    rows = side * side * imgs
    node_id = lax.axis_index("node")
    local_id = lax.axis_index("local")
    z, c = node_id // 2, node_id % 2
    y, x = local_id // 2, local_id % 2

    def scalars(*values):
        return jnp.stack([jnp.asarray(v, jnp.int32) for v in values])

    xt = jnp.transpose(images, (1, 2, 0, 3))
    x_own, x_other = pl.pallas_call(
        split_kernel,
        out_shape=(f32(rows, width), f32(rows, width)),
        in_specs=[SM, HB],
        out_specs=(HB, HB),
        scratch_shapes=[
            pltpu.VMEM((side, rows // side, channels), jnp.float32),
            pltpu.VMEM((2 * side, rows // side, width), jnp.float32),
            pltpu.SemaphoreType.DMA((side,)),
            pltpu.SemaphoreType.DMA((2 * side,)),
        ],
        name="split_images",
    )(scalars(y), xt.reshape(rows, channels))
    x_y = hop(x_other, lambda z, c, y, x: (z, c, 1 - y, x))
    x_x = hop(x_own, lambda z, c, y, x: (z, c, y, 1 - x))
    x_d = hop(x_other, lambda z, c, y, x: (z, c, 1 - y, 1 - x))

    tt = jnp.transpose(targets, (1, 2, 0, 3)).reshape(rows, channels)
    taps = weight.shape[0] * weight.shape[1]
    whole = lambda *shape: pl.BlockSpec(shape, lambda t: (0,) * len(shape))
    r_own, r_other = pl.pallas_call(
        residual_kernel,
        grid=(taps,),
        out_shape=(f32(rows, width), f32(rows, width)),
        in_specs=[
            SM,
            whole(side, side, imgs, channels),
            whole(rows, channels),
            pl.BlockSpec((1, channels, channels), lambda t: (t, 0, 0)),
        ],
        out_specs=(whole(rows, width), whole(rows, width)),
        scratch_shapes=[
            pltpu.VMEM((side + 2, side + 2, imgs, channels), jnp.float32),
            pltpu.VMEM((rows, channels), jnp.float32),
        ],
        cost_estimate=pl.CostEstimate(
            flops=6 * rows * taps * channels * channels, bytes_accessed=4 * taps * channels * channels, transcendentals=0
        ),
        name="residual",
    )(scalars(x), xt, tt, weight.reshape(taps, channels, channels))
    r_x = hop(r_other, lambda z, c, y, x: (z, c, y, 1 - x))
    r_d = hop(r_other, lambda z, c, y, x: (z, c, 1 - y, 1 - x))
    r_y = hop(r_own, lambda z, c, y, x: (z, c, 1 - y, x))

    z_count = lax.axis_size("node") // 2
    part = taps * width // 8
    count = 2 * z_count
    place = scalars(z // 2, x, y)
    keep, send = pl.pallas_call(
        lambda *refs: gradient_kernel(1.0 / rows, side, *refs),
        out_shape=(f32(count, part, 128), f32(count, part, 128)),
        in_specs=[SM] + [HB] * 8,
        out_specs=(VM, VM),
        scratch_shapes=[
            pltpu.VMEM((8, rows, width), jnp.float32),
            pltpu.VMEM((side, width, 3 * (side + 1) * 4 * imgs), jnp.bfloat16),
            pltpu.VMEM((side, side + 3, 4 * imgs, width), jnp.bfloat16),
            pltpu.VMEM((side, side + 3, 4 * imgs, width), jnp.bfloat16),
            pltpu.VMEM((taps * width // BLK, BLK, width), jnp.float32),
            pltpu.SemaphoreType.DMA((8,)),
        ],
        cost_estimate=pl.CostEstimate(
            flops=24 * rows * taps * width * width, bytes_accessed=4 * taps * width * width, transcendentals=0
        ),
        compiler_params=pltpu.CompilerParams(vmem_limit_bytes=FULL),
        name="gradient",
    )(scalars(c, z // 2, y, z % 2), x_own, x_x, x_y, x_d, r_own, r_x, r_y, r_d)

    received = hop(send, lambda z, c, y, x: (z, 1 - c, y, x))
    totals = pl.pallas_call(
        pair_dots_kernel,
        out_shape=f32(8, 128),
        in_specs=[SM, HB, HB],
        out_specs=VM,
        scratch_shapes=[pltpu.VMEM((2 * count, part, 128), jnp.float32), pltpu.SemaphoreType.DMA((2 * count,))],
        compiler_params=pltpu.CompilerParams(vmem_limit_bytes=FULL),
        name="pair_dots",
    )(scalars(c), keep, received)
    totals = plane_sum(totals)
    blocks = pl.pallas_call(
        pair_mix_kernel,
        out_shape=(f32(part, 128),) * count,
        in_specs=[SM] + [VM] * 4 + [HB, HB],
        out_specs=(HB,) * count,
        scratch_shapes=[
            pltpu.VMEM((2 * count, part, 128), jnp.float32),
            pltpu.SemaphoreType.DMA((2 * count,)),
            pltpu.SemaphoreType.DMA((count,)),
        ],
        compiler_params=pltpu.CompilerParams(vmem_limit_bytes=FULL),
        name="pair_mix",
    )(scalars(c), *totals, keep, received)

    moved = []
    for index in range(count):
        e, dy, dx = index // 4, index // 2 % 2, index % 2
        mapping = lambda z, c, y, x, e=e, dy=dy, dx=dx: (2 * (z // 2 ^ e) + c, x, y ^ dy, z % 2 ^ dx)
        moved.append(hop(blocks[index], mapping))
    gram = pl.pallas_call(
        gram_kernel,
        out_shape=f32(16, 128),
        in_specs=[SM] + [HB] * count,
        out_specs=VM,
        scratch_shapes=[pltpu.VMEM((count, part, 128), jnp.float32), pltpu.SemaphoreType.DMA((count,))],
        compiler_params=pltpu.CompilerParams(vmem_limit_bytes=FULL),
        name="gram",
    )(place, *moved)
    along = [hop(gram, lambda z, c, y, x, d=d: (z ^ d, c, y, x)) for d in range(1, z_count)]
    gram = plane_sum((gram + along[0]) + (along[1] + along[2]))
    out = pl.pallas_call(
        place_kernel,
        out_shape=f32(HALF, 4 * part),
        in_specs=[SM] + [VM] * 4 + [HB] * count,
        out_specs=VM,
        scratch_shapes=[
            pltpu.VMEM((count, part, 128), jnp.float32),
            pltpu.VMEM((2 * part // HALF, 2, HALF, HALF), jnp.float32),
            pltpu.SemaphoreType.DMA((count,)),
        ],
        compiler_params=pltpu.CompilerParams(vmem_limit_bytes=FULL),
        name="place",
    )(place, *gram, *moved)
    return out.T


def plane_sum(value):
    value = value + hop(value, lambda z, c, y, x: (z, 1 - c, y, x))
    across = [hop(value, lambda z, c, y, x, d=d: (z, c, y ^ (d >> 1), x ^ (d & 1))) for d in (1, 2, 3)]
    return [value] + across


def fits(images, mesh):
    return (
        mesh.shape["local"] == 4
        and mesh.shape["node"] == 8
        and images.shape[3] == mesh.shape["node"] * HALF
        and images.shape[0] // mesh.size == 8
    )


def solution(mesh):
    def run(images, targets, weight):
        tiled = fits(images, mesh)
        step = jax.shard_map(
            tile_plan if tiled else general_plan,
            mesh=mesh,
            in_specs=(
                P(("node", "local"), None, None, None),
                P(("node", "local"), None, None, None),
                P(),
            ),
            out_specs=P("local", "node"),
            check_vma=False,
        )
        return step(images, targets, weight)

    return run
```

```python
import jax
import jax.numpy as jnp
from jax import lax
from jax.experimental import pallas as pl
from jax.experimental.pallas import tpu as pltpu
from jax.sharding import PartitionSpec as P


epsilon = 1e-06
HALF = 64
BLK = 32
AHEAD = 2
SHARED = 24 * 2**20
ALONE = 65 * 2**20


def partner(value, axis, distance):
    mask = 2**distance
    pairs = [(source, source ^ mask) for source in range(lax.axis_size(axis))]
    return lax.ppermute(value, axis, pairs)


def make_patches(images):
    side = images.shape[1]
    padded = jnp.pad(images, ((0, 0), (1, 1), (1, 1), (0, 0)))
    tap_views = []
    for row_shift in range(3):
        for col_shift in range(3):
            tap_views.append(padded[:, row_shift : row_shift + side, col_shift : col_shift + side, :])
    joined = jnp.concatenate(tap_views, axis=-1)
    return joined.reshape(-1, 9 * images.shape[3])


def adasum_pair(left_vec, right_vec, cross_sum, left_sq, right_sq):
    left_coef = 1.0 - cross_sum / (2.0 * (left_sq + epsilon))
    right_coef = 1.0 - cross_sum / (2.0 * (right_sq + epsilon))
    return left_coef * left_vec + right_coef * right_vec


def general_plan(images, targets, weight):
    channels = images.shape[3]
    flat_w = weight.reshape(9 * channels, channels)
    patches = make_patches(images)
    outputs = jnp.dot(patches, flat_w, precision=lax.Precision.HIGHEST, preferred_element_type=jnp.float32)
    residual = outputs - targets.reshape(-1, channels)
    row_scale = 1.0 / patches.shape[0]
    product = lax.dot_general(
        patches,
        residual,
        (((0,), (0,)), ((), ())),
        precision=lax.Precision.HIGHEST,
        preferred_element_type=jnp.float32,
    )
    my_rows = lax.psum_scatter(product * row_scale, "local", scatter_dimension=0, tiled=True)
    node_count = lax.axis_size("node")
    levels = node_count.bit_length() - 1
    row_count = my_rows.shape[0]
    col_width = channels // node_count
    node_id = lax.axis_index("node")
    piece_blocks = my_rows.reshape(row_count, node_count, col_width)
    for tree_level in range(levels):
        is_upper = jnp.bitwise_and(jnp.right_shift(node_id, tree_level), 1) == 1
        remaining = piece_blocks.shape[1]
        split_view = piece_blocks.reshape(row_count, remaining // 2, 2, col_width)
        lower_half = split_view[:, :, 0, :]
        upper_half = split_view[:, :, 1, :]
        kept_part = jnp.where(is_upper, upper_half, lower_half)
        sent_part = jnp.where(is_upper, lower_half, upper_half)
        received = partner(sent_part, "node", tree_level)
        first_part = jnp.where(is_upper, received, kept_part)
        second_part = jnp.where(is_upper, kept_part, received)
        totals = jnp.stack(
            [
                jnp.sum(first_part * second_part),
                jnp.sum(first_part * first_part),
                jnp.sum(second_part * second_part),
            ]
        )
        totals = lax.psum(totals, "local")
        for inner_bit in range(tree_level + 1):
            totals = totals + partner(totals, "node", inner_bit)
        piece_blocks = adasum_pair(first_part, second_part, totals[0], totals[1], totals[2])
    return piece_blocks.reshape(row_count, col_width)


def hop(value, mapping):
    z_count = lax.axis_size("node") // 2
    pairs = []
    for z in range(z_count):
        for c in range(2):
            for y in range(2):
                for x in range(2):
                    tz, tc, ty, tx = mapping(z, c, y, x)
                    pairs.append((((z * 2 + c) * 2 + y) * 2 + x, ((tz * 2 + tc) * 2 + ty) * 2 + tx))
    return lax.ppermute(value, ("node", "local"), pairs)


def split2(v):
    hi = v.astype(jnp.bfloat16)
    lo = (v - hi.astype(jnp.float32)).astype(jnp.bfloat16)
    return hi, lo


def mm(a, b):
    return jnp.dot(a, b, preferred_element_type=jnp.float32)


def low_lanes(shape):
    return lax.broadcasted_iota(jnp.int32, shape, len(shape) - 1) < HALF


def pair_pack(a, b):
    low = low_lanes(a.shape)
    axis = a.ndim - 1
    return (jnp.where(low, a, pltpu.roll(b, HALF, axis)), jnp.where(low, pltpu.roll(a, HALF, axis), b))


def lane_halves(v):
    evens, odds = [], []
    for k in range(v.shape[1] // 256):
        e, o = pair_pack(v[:, 256 * k : 256 * k + 128], v[:, 256 * k + 128 : 256 * k + 256])
        evens.append(e)
        odds.append(o)
    return jnp.concatenate(evens, axis=1), jnp.concatenate(odds, axis=1)


def split_kernel(s_ref, x_ref, own_ref, other_ref, buf, halves, in_sems, out_sems):
    strips, strip, _ = buf.shape
    spans = [pl.ds(r * strip, strip) for r in range(strips)]
    copies = fetch([x_ref.at[span] for span in spans], [buf.at[r] for r in range(strips)], in_sems)
    up = s_ref[0] == 1
    stores = []
    for r in range(strips):
        copies[r].wait()
        even, odd = lane_halves(buf[r])
        halves[2 * r] = jnp.where(up, odd, even)
        halves[2 * r + 1] = jnp.where(up, even, odd)
        for k, ref in enumerate((own_ref, other_ref)):
            stores.append(pltpu.make_async_copy(halves.at[2 * r + k], ref.at[spans[r]], out_sems.at[2 * r + k]))
            stores[-1].start()
    for store in stores:
        store.wait()


def residual_kernel(s_ref, x_ref, t_ref, w_ref, own_far, other_far, own_near, other_near, *scratch):
    x_buf, t_buf, w_buf, left_ref, acc_ref, sems, w_sems = scratch
    side = acc_ref.shape[0] - 2
    imgs, cols = acc_ref.shape[2:]
    taps = w_buf.shape[0]
    (x_copy,) = fetch([x_ref], [x_buf], sems)
    fetch([w_ref.at[tap] for tap in range(AHEAD)], [w_buf.at[tap] for tap in range(AHEAD)], w_sems)
    acc_ref[...] = jnp.zeros(acc_ref.shape, jnp.float32)
    x_copy.wait()
    xh, xl = split2(x_buf[...])
    left_ref[...] = jnp.concatenate([xh, xh, xl], axis=1)
    t_copy = pltpu.make_async_copy(t_ref, t_buf, sems.at[1])
    t_copy.start()

    def add_tap(tap, carry):
        pltpu.make_async_copy(w_ref.at[tap], w_buf.at[tap], w_sems.at[tap]).wait()

        @pl.when(tap + AHEAD < taps)
        def _():
            later = tap + AHEAD
            pltpu.make_async_copy(w_ref.at[later], w_buf.at[later], w_sems.at[later]).start()

        wh, wl = split2(w_buf[tap])
        product = mm(left_ref[...], jnp.concatenate([wh, wl, wh], axis=0))
        at = (pl.ds(2 - tap // 3, side), pl.ds(2 - tap % 3, side))
        acc_ref[at] += product.reshape(side, side, imgs, cols)
        return carry

    lax.fori_loop(0, taps, add_tap, 0)
    t_copy.wait()
    total = acc_ref[1 : side + 1, 1 : side + 1].reshape(t_buf.shape) - t_buf[...]
    even, odd = lane_halves(total)
    up, high = s_ref[0] == 1, s_ref[1] == 1
    own, other = jnp.where(up, odd, even), jnp.where(up, even, odd)
    for value, near, far in ((own, own_near, own_far), (other, other_near, other_far)):
        near[...] = jnp.where(high, value[:, 128:], value[:, :128])
        far[...] = jnp.where(high, value[:, :128], value[:, 128:])


def prepare_kernel(side, *refs):
    sources, (out_ref, buf, sems) = refs[:4], refs[4:]
    copies = fetch(sources, [buf.at[i] for i in range(4)], sems)
    _, _, width = buf.shape
    span = out_ref.shape[2] // 2
    for copy in copies:
        copy.wait()
    for r in range(side):
        strip = gather(buf, r, side)
        strip = strip.reshape(-1, width)
        strip = jnp.concatenate([strip, jnp.zeros((span - strip.shape[0], width), jnp.float32)], axis=0)
        xh, xl = split2(strip.T)
        out_ref[r, :, :span] = xh
        out_ref[r, :, span:] = xl


def gather(buf, r, side):
    strip = buf.shape[1] // side
    parts = [buf[i, r * strip : (r + 1) * strip, :].reshape(side, strip // side, -1) for i in range(4)]
    return jnp.concatenate(parts, axis=1)


def gradient_kernel(scale, side, s_ref, xt_ref, *refs):
    sources, (keep_ref, send_ref, buf, rh, rl, g_ref, sems) = refs[:4], refs[4:]
    xt = xt_ref
    copies = fetch(sources, [buf.at[i] for i in range(4)], sems)
    width = buf.shape[2]
    span = xt.shape[2] // 2
    for ref in (rh, rl):
        for edge in (0, side + 1, side + 2):
            ref[:, edge] = jnp.zeros((side,) + ref.shape[2:], jnp.bfloat16)
    for copy in copies:
        copy.wait()
    for r in range(side):
        h, lo = split2(gather(buf, r, side))
        rh[r, 1 : side + 1] = h
        rl[r, 1 : side + 1] = lo
    totals = [None] * 9
    for r in range(side):
        taps = [(i, j) for i in range(3) for j in range(3) if 0 <= r - i + 1 < side]

        def strips(ref):
            return [ref[r - i + 1, 2 - j : 2 - j + side + 1].reshape(span, width) for i, j in taps]

        bh, bl = jnp.concatenate(strips(rh), axis=1), jnp.concatenate(strips(rl), axis=1)
        xh, xl = xt[r, :, :span], xt[r, :, span:]
        product = mm(jnp.concatenate([xh, xh, xl], axis=1), jnp.concatenate([bh, bl, bh], axis=0))
        for n, (i, j) in enumerate(taps):
            piece = product[:, n * width : (n + 1) * width]
            tap = 3 * i + j
            totals[tap] = piece if totals[tap] is None else totals[tap] + piece
    blocks = g_ref.shape[0] // 9
    for tap in range(9):
        g_ref[tap * blocks : (tap + 1) * blocks] = (totals[tap] * scale).reshape(blocks, BLK, width)
    odd = s_ref[0] == 1
    per = g_ref.shape[0] // 8
    for quarter in range(4):
        slot = 2 * jnp.bitwise_xor(quarter // 2, s_ref[1]) + jnp.bitwise_xor(quarter % 2, s_ref[2])
        for m in range(per):
            first, second = pair_pack(g_ref[2 * per * quarter + m], g_ref[2 * per * quarter + per + m])
            keep_ref[slot, m * BLK : (m + 1) * BLK, :] = jnp.where(odd, second, first)
            send_ref[slot, m * BLK : (m + 1) * BLK, :] = jnp.where(odd, first, second)


def column_sums(a, b):
    return jnp.sum((a * b).reshape(-1, a.shape[-1]), axis=0, keepdims=True)


def fetch(sources, slots, sems):
    copies = [pltpu.make_async_copy(src, dst, sems.at[i]) for i, (src, dst) in enumerate(zip(sources, slots))]
    for copy in copies:
        copy.start()
    return copies


def pair_dots_kernel(s_ref, keep_ref, received_ref, *refs):
    out_ref, buf, sems = refs[-3:]
    core = s_ref[0]
    count = keep_ref.shape[0]
    sources = [ref.at[d] for d in range(count) for ref in (keep_ref, received_ref)]
    copies = fetch(sources, [buf.at[i] for i in range(2 * count)], sems)
    cross = mine = theirs = jnp.zeros((1, out_ref.shape[1]), jnp.float32)
    for d in range(count):
        copies[2 * d].wait()
        copies[2 * d + 1].wait()
        a, b = buf[2 * d], buf[2 * d + 1]
        cross += column_sums(a, b)
        mine += column_sums(a, a)
        theirs += column_sums(b, b)
    left, right = jnp.where(core == 0, mine, theirs), jnp.where(core == 0, theirs, mine)
    if len(refs) > 3:
        before = refs[0]
        cross, left, right = cross + before[0:1], left + before[1:2], right + before[2:3]
    out_ref[...] = jnp.zeros(out_ref.shape, jnp.float32)
    out_ref[0:1] = cross
    out_ref[1:2] = left
    out_ref[2:3] = right


def pair_coefs(cross, left_sq, right_sq):
    return 1.0 - cross / (2.0 * (left_sq + epsilon)), 1.0 - cross / (2.0 * (right_sq + epsilon))


def pair_mix_kernel(s_ref, t0, t1, t2, t3, keep_ref, received_ref, *refs):
    core = s_ref[0]
    count = keep_ref.shape[0]
    out_refs, (buf, sums, in_sems, out_sems) = refs[:count], refs[count:]
    order = list(range(count - 1, -1, -1))
    slots = [sums.at[i] for i in range(4)] + [buf.at[i] for i in range(2 * count)]
    copies = fetch([t0, t1, t2, t3] + [ref.at[d] for d in order for ref in (keep_ref, received_ref)], slots, in_sems)
    for copy in copies[:4]:
        copy.wait()
    totals = jnp.sum((sums[0] + sums[1]) + (sums[2] + sums[3]), axis=1, keepdims=True)
    left, right = pair_coefs(totals[0:1], totals[1:2], totals[2:3])
    keep_coef = jnp.where(core == 0, left, right)
    received_coef = jnp.where(core == 0, right, left)
    stores = []
    for i, d in enumerate(order):
        copies[4 + 2 * i].wait()
        copies[5 + 2 * i].wait()
        buf[2 * i] = keep_coef * buf[2 * i] + received_coef * buf[2 * i + 1]
        stores.append(pltpu.make_async_copy(buf.at[2 * i], out_refs[d], out_sems.at[i]))
        stores[-1].start()
    for store in stores:
        store.wait()


def gram_kernel(s_ref, *refs):
    upper, x = s_ref[0], s_ref[1]
    blocks, (gram_ref, buf, sems) = refs[:8], refs[8:]
    copies = fetch(blocks, [buf.at[slot_of(i)] for i in range(8)], sems)
    node = [2 * jnp.bitwise_xor(upper, d // 2) + jnp.bitwise_xor(x, d % 2) for d in range(4)]
    for i in (0, 1, 2, 3, 4, 5, 6, 7):
        copies[i].wait()
    for e in range(4):
        for d in range(e + 1):
            value = column_sums(buf[2 * d : 2 * d + 2], buf[2 * e : 2 * e + 2])
            gram_ref[pl.ds(4 * node[d] + node[e], 1)] = value
            gram_ref[pl.ds(4 * node[e] + node[d], 1)] = value


def slot_of(index):
    e, dy, dx = index // 4, index // 2 % 2, index % 2
    return 4 * e + 2 * dx + dy


def place_kernel(s_ref, *refs):
    upper, x, y = s_ref[0], s_ref[1], s_ref[2]
    sources, (out_ref, parts, sums, rows_ref, sems) = refs[:12], refs[12:]
    slots = [sums.at[i] for i in range(4)] + [parts.at[slot_of(i)] for i in range(8)]
    copies = fetch(sources, slots, sems)
    for copy in copies[:4]:
        copy.wait()
    gram = jnp.sum((sums[0] + sums[1]) + (sums[2] + sums[3]), axis=1, keepdims=True)
    g = lambda a, b: gram[4 * a + b : 4 * a + b + 1]
    p = pair_coefs(g(0, 1), g(0, 0), g(1, 1)) + pair_coefs(g(2, 3), g(2, 2), g(3, 3))
    cross = p[0] * (p[2] * g(0, 2) + p[3] * g(0, 3)) + p[1] * (p[2] * g(1, 2) + p[3] * g(1, 3))
    near = p[0] * p[0] * g(0, 0) + 2.0 * p[0] * p[1] * g(0, 1) + p[1] * p[1] * g(1, 1)
    far = p[2] * p[2] * g(2, 2) + 2.0 * p[2] * p[3] * g(2, 3) + p[3] * p[3] * g(3, 3)
    near_coef, far_coef = pair_coefs(cross, near, far)
    absolute = (near_coef * p[0], near_coef * p[1], far_coef * p[2], far_coef * p[3])
    coefs = []
    for d in range(4):
        owner = 2 * jnp.bitwise_xor(upper, d // 2) + jnp.bitwise_xor(x, d % 2)
        coef = absolute[3]
        for a in range(3):
            coef = jnp.where(owner == a, absolute[a], coef)
        coefs.append(coef)
    for copy in copies[4:]:
        copy.wait()
    for dy in range(2):
        part = [parts[2 * d + dy] for d in range(4)]
        block = coefs[0] * part[0] + coefs[1] * part[1] + (coefs[2] * part[2] + coefs[3] * part[3])
        upper_half = pltpu.roll(block, HALF, 1)
        rows = jnp.concatenate([block[:, :HALF], upper_half[:, :HALF]], axis=0)
        rows = rows.reshape(rows_ref.shape[0], HALF, HALF)
        slot = jnp.bitwise_xor(y, dy)
        for k in range(rows_ref.shape[0]):
            rows_ref[k, slot] = rows[k]
    out_ref[...] = rows_ref[...].reshape(out_ref.shape[1], HALF).T


VM = pl.BlockSpec(memory_space=pltpu.VMEM)
HB = pl.BlockSpec(memory_space=pltpu.HBM)
SM = pl.BlockSpec(memory_space=pltpu.SMEM)


def f32(*shape):
    return jax.ShapeDtypeStruct(shape, jnp.float32)


def tile_plan(images, targets, weight):
    return tiles(images, targets, weight)


def tiles(images, targets, weight):
    imgs, side, _, channels = images.shape
    width = channels // 2
    rows = side * side * imgs
    node_id = lax.axis_index("node")
    local_id = lax.axis_index("local")
    z, c = node_id // 2, node_id % 2
    y, x = local_id // 2, local_id % 2

    def scalars(*values):
        return jnp.stack([jnp.asarray(v, jnp.int32) for v in values])

    xt = jnp.transpose(images, (1, 2, 0, 3))
    x_own, x_other = pl.pallas_call(
        split_kernel,
        out_shape=(f32(rows, width), f32(rows, width)),
        in_specs=[SM, HB],
        out_specs=(HB, HB),
        scratch_shapes=[
            pltpu.VMEM((side, rows // side, channels), jnp.float32),
            pltpu.VMEM((2 * side, rows // side, width), jnp.float32),
            pltpu.SemaphoreType.DMA((side,)),
            pltpu.SemaphoreType.DMA((2 * side,)),
        ],
        compiler_params=pltpu.CompilerParams(vmem_limit_bytes=ALONE),
        name="split_images",
    )(scalars(y), xt.reshape(rows, channels))
    x_y = hop(x_other, lambda z, c, y, x: (z, c, 1 - y, x))
    x_x = hop(x_own, lambda z, c, y, x: (z, c, y, 1 - x))
    x_d = hop(x_other, lambda z, c, y, x: (z, c, 1 - y, 1 - x))

    tt = jnp.transpose(targets, (1, 2, 0, 3)).reshape(rows, channels)
    taps = weight.shape[0] * weight.shape[1]
    own_far, other_far, own_near, other_near = pl.pallas_call(
        residual_kernel,
        out_shape=(f32(rows, 128),) * 4,
        in_specs=[SM] + [HB] * 3,
        out_specs=(VM,) * 4,
        scratch_shapes=[
            pltpu.VMEM((rows, channels), jnp.float32),
            pltpu.VMEM((rows, channels), jnp.float32),
            pltpu.VMEM((taps, channels, channels), jnp.float32),
            pltpu.VMEM((rows, 3 * channels), jnp.bfloat16),
            pltpu.VMEM((side + 2, side + 2, imgs, channels), jnp.float32),
            pltpu.SemaphoreType.DMA((2,)),
            pltpu.SemaphoreType.DMA((taps,)),
        ],
        cost_estimate=pl.CostEstimate(
            flops=6 * rows * taps * channels * channels, bytes_accessed=4 * taps * channels * channels, transcendentals=0
        ),
        compiler_params=pltpu.CompilerParams(vmem_limit_bytes=ALONE),
        name="residual",
    )(scalars(x, z // 2), xt.reshape(rows, channels), tt, weight.reshape(taps, channels, channels))
    far = exchange(own_far, other_far)
    near = exchange(own_near, other_near)

    span = (side + 1) * 4 * imgs
    xt_shape = (side, width, 2 * span)
    images_t = pl.pallas_call(
        lambda *refs: prepare_kernel(side, *refs),
        out_shape=jax.ShapeDtypeStruct(xt_shape, jnp.bfloat16),
        in_specs=[HB] * 4,
        out_specs=VM,
        scratch_shapes=[pltpu.VMEM((4, rows, width), jnp.float32), pltpu.SemaphoreType.DMA((4,))],
        compiler_params=pltpu.CompilerParams(vmem_limit_bytes=SHARED),
        name="prepare",
    )(x_own, x_x, x_y, x_d)

    z_count = lax.axis_size("node") // 2
    part = taps * width // 8
    count = 2 * z_count
    half = count // 2
    place = scalars(z // 2, x, y)

    def gradient(pieces):
        return pl.pallas_call(
            lambda *refs: gradient_kernel(1.0 / rows, side, *refs),
            out_shape=(f32(half, part, 128), f32(half, part, 128)),
            in_specs=[SM, VM] + [HB] * 4,
            out_specs=(VM, VM),
            scratch_shapes=[
                pltpu.VMEM((4, rows, 128), jnp.float32),
                pltpu.VMEM((side, side + 3, 4 * imgs, 128), jnp.bfloat16),
                pltpu.VMEM((side, side + 3, 4 * imgs, 128), jnp.bfloat16),
                pltpu.VMEM((taps * width // BLK, BLK, 128), jnp.float32),
                pltpu.SemaphoreType.DMA((4,)),
            ],
            cost_estimate=pl.CostEstimate(
                flops=24 * rows * taps * width * 128, bytes_accessed=4 * taps * width * 128, transcendentals=0
            ),
            compiler_params=pltpu.CompilerParams(vmem_limit_bytes=SHARED),
        )(scalars(c, y, z % 2), images_t, *pieces)

    def dots(keep, received, before):
        return pl.pallas_call(
            pair_dots_kernel,
            out_shape=f32(8, 128),
            in_specs=[SM, HB, HB] + [VM] * len(before),
            out_specs=VM,
            scratch_shapes=[pltpu.VMEM((2 * half, part, 128), jnp.float32), pltpu.SemaphoreType.DMA((2 * half,))],
            compiler_params=pltpu.CompilerParams(vmem_limit_bytes=SHARED),
        )(scalars(c), keep, received, *before)

    across = lambda z, c, y, x: (z, 1 - c, y, x)
    keep_far, send_far = gradient(far)
    received_far = hop(send_far, across)
    keep_near, send_near = gradient(near)
    received_near = hop(send_near, across)
    totals = dots(keep_far, received_far, ())
    totals = plane_sum(dots(keep_near, received_near, (totals,)))

    def mix(keep, received):
        return pl.pallas_call(
            pair_mix_kernel,
            out_shape=(f32(part, 128),) * half,
            in_specs=[SM] + [HB] * 6,
            out_specs=(HB,) * half,
            scratch_shapes=[
                pltpu.VMEM((2 * half, part, 128), jnp.float32),
                pltpu.VMEM((4, 8, 128), jnp.float32),
                pltpu.SemaphoreType.DMA((4 + 2 * half,)),
                pltpu.SemaphoreType.DMA((half,)),
            ],
            compiler_params=pltpu.CompilerParams(vmem_limit_bytes=SHARED),
        )(scalars(c), *totals, keep, received)

    mixed_far = mix(keep_far, received_far)
    blocks = tuple(mix(keep_near, received_near)) + tuple(mixed_far)

    moved = []
    for index in range(count):
        e, dy, dx = index // 4, index // 2 % 2, index % 2
        mapping = lambda z, c, y, x, e=e, dy=dy, dx=dx: (2 * (z // 2 ^ e) + c, x, y ^ dy, z % 2 ^ dx)
        moved.append(hop(blocks[index], mapping))
    gram = pl.pallas_call(
        gram_kernel,
        out_shape=f32(16, 128),
        in_specs=[SM] + [HB] * count,
        out_specs=VM,
        scratch_shapes=[pltpu.VMEM((count, part, 128), jnp.float32), pltpu.SemaphoreType.DMA((count,))],
        compiler_params=pltpu.CompilerParams(vmem_limit_bytes=SHARED),
        name="gram",
    )(place, *moved)
    along = [hop(gram, lambda z, c, y, x, d=d: (z ^ d, c, y, x)) for d in range(1, z_count)]
    gram = plane_sum((gram + along[0]) + (along[1] + along[2]))
    out = pl.pallas_call(
        place_kernel,
        out_shape=f32(HALF, 4 * part),
        in_specs=[SM] + [HB] * (4 + count),
        out_specs=VM,
        scratch_shapes=[
            pltpu.VMEM((count, part, 128), jnp.float32),
            pltpu.VMEM((4, 16, 128), jnp.float32),
            pltpu.VMEM((2 * part // HALF, 2, HALF, HALF), jnp.float32),
            pltpu.SemaphoreType.DMA((4 + count,)),
        ],
        compiler_params=pltpu.CompilerParams(vmem_limit_bytes=SHARED),
        name="place",
    )(place, *gram, *moved)
    return out.T


def exchange(own, other):
    along_x = hop(other, lambda z, c, y, x: (z, c, y, 1 - x))
    across = hop(other, lambda z, c, y, x: (z, c, 1 - y, 1 - x))
    along_y = hop(own, lambda z, c, y, x: (z, c, 1 - y, x))
    return own, along_x, along_y, across


def plane_sum(value):
    value = value + hop(value, lambda z, c, y, x: (z, 1 - c, y, x))
    across = [hop(value, lambda z, c, y, x, d=d: (z, c, y ^ (d >> 1), x ^ (d & 1))) for d in (1, 2, 3)]
    return [value] + across


def fits(images, mesh):
    return (
        mesh.shape["local"] == 4
        and mesh.shape["node"] == 8
        and images.shape[3] == mesh.shape["node"] * HALF
        and images.shape[0] // mesh.size == 8
    )


def solution(mesh):
    def run(images, targets, weight):
        tiled = fits(images, mesh)
        step = jax.shard_map(
            tile_plan if tiled else general_plan,
            mesh=mesh,
            in_specs=(
                P(("node", "local"), None, None, None),
                P(("node", "local"), None, None, None),
                P(),
            ),
            out_specs=P("local", "node"),
            check_vma=False,
        )
        return step(images, targets, weight)

    return run
```

```python
import jax
import jax.numpy as jnp
from jax import lax
from jax.experimental import pallas as pl
from jax.experimental.pallas import tpu as pltpu
from jax.sharding import PartitionSpec as P


epsilon = 1e-06
HALF = 64
BLK = 32
AHEAD = 2
SHARED = 24 * 2**20
ALONE = 65 * 2**20


def partner(value, axis, distance):
    mask = 2**distance
    pairs = [(source, source ^ mask) for source in range(lax.axis_size(axis))]
    return lax.ppermute(value, axis, pairs)


def make_patches(images):
    side = images.shape[1]
    padded = jnp.pad(images, ((0, 0), (1, 1), (1, 1), (0, 0)))
    tap_views = []
    for row_shift in range(3):
        for col_shift in range(3):
            tap_views.append(padded[:, row_shift : row_shift + side, col_shift : col_shift + side, :])
    joined = jnp.concatenate(tap_views, axis=-1)
    return joined.reshape(-1, 9 * images.shape[3])


def adasum_pair(left_vec, right_vec, cross_sum, left_sq, right_sq):
    left_coef = 1.0 - cross_sum / (2.0 * (left_sq + epsilon))
    right_coef = 1.0 - cross_sum / (2.0 * (right_sq + epsilon))
    return left_coef * left_vec + right_coef * right_vec


def general_plan(images, targets, weight):
    channels = images.shape[3]
    flat_w = weight.reshape(9 * channels, channels)
    patches = make_patches(images)
    outputs = jnp.dot(patches, flat_w, precision=lax.Precision.HIGHEST, preferred_element_type=jnp.float32)
    residual = outputs - targets.reshape(-1, channels)
    row_scale = 1.0 / patches.shape[0]
    product = lax.dot_general(
        patches,
        residual,
        (((0,), (0,)), ((), ())),
        precision=lax.Precision.HIGHEST,
        preferred_element_type=jnp.float32,
    )
    my_rows = lax.psum_scatter(product * row_scale, "local", scatter_dimension=0, tiled=True)
    node_count = lax.axis_size("node")
    levels = node_count.bit_length() - 1
    row_count = my_rows.shape[0]
    col_width = channels // node_count
    node_id = lax.axis_index("node")
    piece_blocks = my_rows.reshape(row_count, node_count, col_width)
    for tree_level in range(levels):
        is_upper = jnp.bitwise_and(jnp.right_shift(node_id, tree_level), 1) == 1
        remaining = piece_blocks.shape[1]
        split_view = piece_blocks.reshape(row_count, remaining // 2, 2, col_width)
        lower_half = split_view[:, :, 0, :]
        upper_half = split_view[:, :, 1, :]
        kept_part = jnp.where(is_upper, upper_half, lower_half)
        sent_part = jnp.where(is_upper, lower_half, upper_half)
        received = partner(sent_part, "node", tree_level)
        first_part = jnp.where(is_upper, received, kept_part)
        second_part = jnp.where(is_upper, kept_part, received)
        totals = jnp.stack(
            [
                jnp.sum(first_part * second_part),
                jnp.sum(first_part * first_part),
                jnp.sum(second_part * second_part),
            ]
        )
        totals = lax.psum(totals, "local")
        for inner_bit in range(tree_level + 1):
            totals = totals + partner(totals, "node", inner_bit)
        piece_blocks = adasum_pair(first_part, second_part, totals[0], totals[1], totals[2])
    return piece_blocks.reshape(row_count, col_width)


def hop(value, mapping):
    z_count = lax.axis_size("node") // 2
    pairs = []
    for z in range(z_count):
        for c in range(2):
            for y in range(2):
                for x in range(2):
                    tz, tc, ty, tx = mapping(z, c, y, x)
                    pairs.append((((z * 2 + c) * 2 + y) * 2 + x, ((tz * 2 + tc) * 2 + ty) * 2 + tx))
    return lax.ppermute(value, ("node", "local"), pairs)


def split2(v):
    hi = v.astype(jnp.bfloat16)
    lo = (v - hi.astype(jnp.float32)).astype(jnp.bfloat16)
    return hi, lo


def mm(a, b):
    return jnp.dot(a, b, preferred_element_type=jnp.float32)


def low_lanes(shape):
    return lax.broadcasted_iota(jnp.int32, shape, len(shape) - 1) < HALF


def pair_pack(a, b):
    low = low_lanes(a.shape)
    axis = a.ndim - 1
    return (jnp.where(low, a, pltpu.roll(b, HALF, axis)), jnp.where(low, pltpu.roll(a, HALF, axis), b))


def lane_halves(v):
    evens, odds = [], []
    for k in range(v.shape[1] // 256):
        e, o = pair_pack(v[:, 256 * k : 256 * k + 128], v[:, 256 * k + 128 : 256 * k + 256])
        evens.append(e)
        odds.append(o)
    return jnp.concatenate(evens, axis=1), jnp.concatenate(odds, axis=1)


def split_kernel(s_ref, x_ref, own_ref, other_ref, buf, halves, in_sems, out_sems):
    strips, strip, _ = buf.shape
    spans = [pl.ds(r * strip, strip) for r in range(strips)]
    copies = fetch([x_ref.at[span] for span in spans], [buf.at[r] for r in range(strips)], in_sems)
    up = s_ref[0] == 1
    stores = []
    for r in range(strips):
        copies[r].wait()
        even, odd = lane_halves(buf[r])
        halves[2 * r] = jnp.where(up, odd, even)
        halves[2 * r + 1] = jnp.where(up, even, odd)
        for k, ref in enumerate((own_ref, other_ref)):
            stores.append(pltpu.make_async_copy(halves.at[2 * r + k], ref.at[spans[r]], out_sems.at[2 * r + k]))
            stores[-1].start()
    for store in stores:
        store.wait()


def residual_kernel(s_ref, x_ref, t_ref, w_ref, own_far, other_far, own_near, other_near, *scratch):
    x_buf, t_buf, w_buf, left_ref, acc_ref, sems, w_sems = scratch
    side = acc_ref.shape[0] - 2
    imgs, cols = acc_ref.shape[2:]
    taps = w_buf.shape[0]
    (x_copy,) = fetch([x_ref], [x_buf], sems)
    fetch([w_ref.at[tap] for tap in range(AHEAD)], [w_buf.at[tap] for tap in range(AHEAD)], w_sems)
    acc_ref[...] = jnp.zeros(acc_ref.shape, jnp.float32)
    x_copy.wait()
    xh, xl = split2(x_buf[...])
    left_ref[...] = jnp.concatenate([xh, xh, xl], axis=1)
    t_copy = pltpu.make_async_copy(t_ref, t_buf, sems.at[1])
    t_copy.start()

    def add_tap(tap, carry):
        pltpu.make_async_copy(w_ref.at[tap], w_buf.at[tap], w_sems.at[tap]).wait()

        @pl.when(tap + AHEAD < taps)
        def _():
            later = tap + AHEAD
            pltpu.make_async_copy(w_ref.at[later], w_buf.at[later], w_sems.at[later]).start()

        wh, wl = split2(w_buf[tap])
        product = mm(left_ref[...], jnp.concatenate([wh, wl, wh], axis=0))
        at = (pl.ds(2 - tap // 3, side), pl.ds(2 - tap % 3, side))
        acc_ref[at] += product.reshape(side, side, imgs, cols)
        return carry

    lax.fori_loop(0, taps, add_tap, 0)
    t_copy.wait()
    total = acc_ref[1 : side + 1, 1 : side + 1].reshape(t_buf.shape) - t_buf[...]
    even, odd = lane_halves(total)
    up, high = s_ref[0] == 1, s_ref[1] == 1
    own, other = jnp.where(up, odd, even), jnp.where(up, even, odd)
    for value, near, far in ((own, own_near, own_far), (other, other_near, other_far)):
        near[...] = jnp.where(high, value[:, 128:], value[:, :128])
        far[...] = jnp.where(high, value[:, :128], value[:, 128:])


def prepare_kernel(side, *refs):
    sources, (out_ref, buf, sems) = refs[:4], refs[4:]
    copies = fetch(sources, [buf.at[i] for i in range(4)], sems)
    _, _, width = buf.shape
    span = out_ref.shape[2] // 2
    for copy in copies:
        copy.wait()
    for r in range(side):
        strip = gather([buf.at[i] for i in range(4)], r, side)
        strip = strip.reshape(-1, width)
        strip = jnp.concatenate([strip, jnp.zeros((span - strip.shape[0], width), jnp.float32)], axis=0)
        xh, xl = split2(strip.T)
        out_ref[r, :, :span] = xh
        out_ref[r, :, span:] = xl


def gather(refs, r, side):
    strip = refs[0].shape[0] // side
    parts = [ref[r * strip : (r + 1) * strip, :].reshape(side, strip // side, -1) for ref in refs]
    return jnp.concatenate(parts, axis=1)


def gradient_kernel(scale, side, s_ref, xt_ref, *refs):
    sources, (keep_ref, send_ref, rh, rl, g_ref) = refs[:4], refs[4:]
    xt = xt_ref
    width = sources[0].shape[1]
    span = xt.shape[2] // 2
    for ref in (rh, rl):
        for edge in (0, side + 1, side + 2):
            ref[:, edge] = jnp.zeros((side,) + ref.shape[2:], jnp.bfloat16)
    for r in range(side):
        h, lo = split2(gather(sources, r, side))
        rh[r, 1 : side + 1] = h
        rl[r, 1 : side + 1] = lo
    totals = [None] * 9
    for r in range(side):
        taps = [(i, j) for i in range(3) for j in range(3) if 0 <= r - i + 1 < side]

        def strips(ref):
            return [ref[r - i + 1, 2 - j : 2 - j + side + 1].reshape(span, width) for i, j in taps]

        bh, bl = jnp.concatenate(strips(rh), axis=1), jnp.concatenate(strips(rl), axis=1)
        xh, xl = xt[r, :, :span], xt[r, :, span:]
        product = mm(jnp.concatenate([xh, xh, xl], axis=1), jnp.concatenate([bh, bl, bh], axis=0))
        for n, (i, j) in enumerate(taps):
            piece = product[:, n * width : (n + 1) * width]
            tap = 3 * i + j
            totals[tap] = piece if totals[tap] is None else totals[tap] + piece
    blocks = g_ref.shape[0] // 9
    for tap in range(9):
        g_ref[tap * blocks : (tap + 1) * blocks] = (totals[tap] * scale).reshape(blocks, BLK, width)
    odd = s_ref[0] == 1
    per = g_ref.shape[0] // 8
    for quarter in range(4):
        slot = 2 * jnp.bitwise_xor(quarter // 2, s_ref[1]) + jnp.bitwise_xor(quarter % 2, s_ref[2])
        for m in range(per):
            first, second = pair_pack(g_ref[2 * per * quarter + m], g_ref[2 * per * quarter + per + m])
            keep_ref[slot, m * BLK : (m + 1) * BLK, :] = jnp.where(odd, second, first)
            send_ref[slot, m * BLK : (m + 1) * BLK, :] = jnp.where(odd, first, second)


def column_sums(a, b):
    return jnp.sum((a * b).reshape(-1, a.shape[-1]), axis=0, keepdims=True)


def fetch(sources, slots, sems):
    copies = [pltpu.make_async_copy(src, dst, sems.at[i]) for i, (src, dst) in enumerate(zip(sources, slots))]
    for copy in copies:
        copy.start()
    return copies


def pair_dots_kernel(s_ref, keep_ref, received_ref, *refs):
    core = s_ref[0]
    out_ref = refs[-1]
    cross = mine = theirs = jnp.zeros((1, out_ref.shape[1]), jnp.float32)
    for d in range(keep_ref.shape[0]):
        a, b = keep_ref[d], received_ref[d]
        cross += column_sums(a, b)
        mine += column_sums(a, a)
        theirs += column_sums(b, b)
    left, right = jnp.where(core == 0, mine, theirs), jnp.where(core == 0, theirs, mine)
    if len(refs) > 1:
        before = refs[0]
        cross, left, right = cross + before[0:1], left + before[1:2], right + before[2:3]
    out_ref[...] = jnp.zeros(out_ref.shape, jnp.float32)
    out_ref[0:1] = cross
    out_ref[1:2] = left
    out_ref[2:3] = right


def pair_coefs(cross, left_sq, right_sq):
    return 1.0 - cross / (2.0 * (left_sq + epsilon)), 1.0 - cross / (2.0 * (right_sq + epsilon))


def sum_four(refs):
    return (refs[0][...] + refs[1][...]) + (refs[2][...] + refs[3][...])


def pair_mix_kernel(s_ref, t0, t1, t2, t3, keep_ref, received_ref, *out_refs):
    core = s_ref[0]
    totals = jnp.sum(sum_four((t0, t1, t2, t3)), axis=1, keepdims=True)
    left, right = pair_coefs(totals[0:1], totals[1:2], totals[2:3])
    keep_coef = jnp.where(core == 0, left, right)
    received_coef = jnp.where(core == 0, right, left)
    for d, out in enumerate(out_refs):
        out[...] = keep_coef * keep_ref[d] + received_coef * received_ref[d]


def gram_kernel(s_ref, *refs):
    upper, x = s_ref[0], s_ref[1]
    blocks, gram_ref = refs[:8], refs[8]
    node = [2 * jnp.bitwise_xor(upper, d // 2) + jnp.bitwise_xor(x, d % 2) for d in range(4)]
    for e in range(4):
        for d in range(e + 1):
            value = sum(column_sums(blocks[slot_of(d, dy)][...], blocks[slot_of(e, dy)][...]) for dy in range(2))
            gram_ref[pl.ds(4 * node[d] + node[e], 1)] = value
            gram_ref[pl.ds(4 * node[e] + node[d], 1)] = value


def slot_of(d, dy):
    return 4 * (d // 2) + 2 * dy + d % 2


def place_kernel(s_ref, *refs):
    upper, x, y = s_ref[0], s_ref[1], s_ref[2]
    blocks, (out_ref, rows_ref) = refs[4:12], refs[12:]
    gram = jnp.sum(sum_four(refs[:4]), axis=1, keepdims=True)
    g = lambda a, b: gram[4 * a + b : 4 * a + b + 1]
    p = pair_coefs(g(0, 1), g(0, 0), g(1, 1)) + pair_coefs(g(2, 3), g(2, 2), g(3, 3))
    cross = p[0] * (p[2] * g(0, 2) + p[3] * g(0, 3)) + p[1] * (p[2] * g(1, 2) + p[3] * g(1, 3))
    near = p[0] * p[0] * g(0, 0) + 2.0 * p[0] * p[1] * g(0, 1) + p[1] * p[1] * g(1, 1)
    far = p[2] * p[2] * g(2, 2) + 2.0 * p[2] * p[3] * g(2, 3) + p[3] * p[3] * g(3, 3)
    near_coef, far_coef = pair_coefs(cross, near, far)
    absolute = (near_coef * p[0], near_coef * p[1], far_coef * p[2], far_coef * p[3])
    coefs = []
    for d in range(4):
        owner = 2 * jnp.bitwise_xor(upper, d // 2) + jnp.bitwise_xor(x, d % 2)
        coef = absolute[3]
        for a in range(3):
            coef = jnp.where(owner == a, absolute[a], coef)
        coefs.append(coef)
    for dy in range(2):
        part = [blocks[slot_of(d, dy)][...] for d in range(4)]
        block = coefs[0] * part[0] + coefs[1] * part[1] + (coefs[2] * part[2] + coefs[3] * part[3])
        upper_half = pltpu.roll(block, HALF, 1)
        rows = jnp.concatenate([block[:, :HALF], upper_half[:, :HALF]], axis=0)
        rows = rows.reshape(rows_ref.shape[0], HALF, HALF)
        slot = jnp.bitwise_xor(y, dy)
        for k in range(rows_ref.shape[0]):
            rows_ref[k, slot] = rows[k]
    out_ref[...] = rows_ref[...].reshape(out_ref.shape[1], HALF).T


VM = pl.BlockSpec(memory_space=pltpu.VMEM)
HB = pl.BlockSpec(memory_space=pltpu.HBM)
SM = pl.BlockSpec(memory_space=pltpu.SMEM)


def f32(*shape):
    return jax.ShapeDtypeStruct(shape, jnp.float32)


def tile_plan(images, targets, weight):
    return tiles(images, targets, weight)


def tiles(images, targets, weight):
    imgs, side, _, channels = images.shape
    width = channels // 2
    rows = side * side * imgs
    node_id = lax.axis_index("node")
    local_id = lax.axis_index("local")
    z, c = node_id // 2, node_id % 2
    y, x = local_id // 2, local_id % 2

    def scalars(*values):
        return jnp.stack([jnp.asarray(v, jnp.int32) for v in values])

    xt = jnp.transpose(images, (1, 2, 0, 3))
    x_own, x_other = pl.pallas_call(
        split_kernel,
        out_shape=(f32(rows, width), f32(rows, width)),
        in_specs=[SM, HB],
        out_specs=(HB, HB),
        scratch_shapes=[
            pltpu.VMEM((side, rows // side, channels), jnp.float32),
            pltpu.VMEM((2 * side, rows // side, width), jnp.float32),
            pltpu.SemaphoreType.DMA((side,)),
            pltpu.SemaphoreType.DMA((2 * side,)),
        ],
        compiler_params=pltpu.CompilerParams(vmem_limit_bytes=ALONE),
        name="split_images",
    )(scalars(y), xt.reshape(rows, channels))
    x_y = hop(x_other, lambda z, c, y, x: (z, c, 1 - y, x))
    x_x = hop(x_own, lambda z, c, y, x: (z, c, y, 1 - x))
    x_d = hop(x_other, lambda z, c, y, x: (z, c, 1 - y, 1 - x))

    tt = jnp.transpose(targets, (1, 2, 0, 3)).reshape(rows, channels)
    taps = weight.shape[0] * weight.shape[1]
    own_far, other_far, own_near, other_near = pl.pallas_call(
        residual_kernel,
        out_shape=(f32(rows, 128),) * 4,
        in_specs=[SM] + [HB] * 3,
        out_specs=(VM,) * 4,
        scratch_shapes=[
            pltpu.VMEM((rows, channels), jnp.float32),
            pltpu.VMEM((rows, channels), jnp.float32),
            pltpu.VMEM((taps, channels, channels), jnp.float32),
            pltpu.VMEM((rows, 3 * channels), jnp.bfloat16),
            pltpu.VMEM((side + 2, side + 2, imgs, channels), jnp.float32),
            pltpu.SemaphoreType.DMA((2,)),
            pltpu.SemaphoreType.DMA((taps,)),
        ],
        cost_estimate=pl.CostEstimate(
            flops=6 * rows * taps * channels * channels, bytes_accessed=4 * taps * channels * channels, transcendentals=0
        ),
        compiler_params=pltpu.CompilerParams(vmem_limit_bytes=ALONE),
        name="residual",
    )(scalars(x, z // 2), xt.reshape(rows, channels), tt, weight.reshape(taps, channels, channels))
    far = exchange(own_far, other_far)
    near = exchange(own_near, other_near)

    span = (side + 1) * 4 * imgs
    xt_shape = (side, width, 2 * span)
    images_t = pl.pallas_call(
        lambda *refs: prepare_kernel(side, *refs),
        out_shape=jax.ShapeDtypeStruct(xt_shape, jnp.bfloat16),
        in_specs=[HB] * 4,
        out_specs=VM,
        scratch_shapes=[pltpu.VMEM((4, rows, width), jnp.float32), pltpu.SemaphoreType.DMA((4,))],
        compiler_params=pltpu.CompilerParams(vmem_limit_bytes=SHARED),
        name="prepare",
    )(x_own, x_x, x_y, x_d)

    z_count = lax.axis_size("node") // 2
    part = taps * width // 8
    count = 2 * z_count
    half = count // 2
    place = scalars(z // 2, x, y)

    def gradient(pieces):
        return pl.pallas_call(
            lambda *refs: gradient_kernel(1.0 / rows, side, *refs),
            out_shape=(f32(half, part, 128), f32(half, part, 128)),
            in_specs=[SM] + [VM] * 5,
            out_specs=(VM, VM),
            scratch_shapes=[
                pltpu.VMEM((side, side + 3, 4 * imgs, 128), jnp.bfloat16),
                pltpu.VMEM((side, side + 3, 4 * imgs, 128), jnp.bfloat16),
                pltpu.VMEM((taps * width // BLK, BLK, 128), jnp.float32),
            ],
            cost_estimate=pl.CostEstimate(
                flops=24 * rows * taps * width * 128, bytes_accessed=4 * taps * width * 128, transcendentals=0
            ),
            compiler_params=pltpu.CompilerParams(vmem_limit_bytes=SHARED),
        )(scalars(c, y, z % 2), images_t, *pieces)

    def dots(keep, received, before):
        return pl.pallas_call(
            pair_dots_kernel,
            out_shape=f32(8, 128),
            in_specs=[SM, VM, VM] + [VM] * len(before),
            out_specs=VM,
            compiler_params=pltpu.CompilerParams(vmem_limit_bytes=SHARED),
        )(scalars(c), keep, received, *before)

    across = lambda z, c, y, x: (z, 1 - c, y, x)
    keep_far, send_far = gradient(far)
    received_far = hop(send_far, across)
    keep_near, send_near = gradient(near)
    received_near = hop(send_near, across)
    totals = dots(keep_far, received_far, ())
    totals = plane_sum(dots(keep_near, received_near, (totals,)))

    def mix(keep, received):
        return pl.pallas_call(
            pair_mix_kernel,
            out_shape=(f32(part, 128),) * half,
            in_specs=[SM] + [VM] * 6,
            out_specs=(VM,) * half,
            compiler_params=pltpu.CompilerParams(vmem_limit_bytes=SHARED),
        )(scalars(c), *totals, keep, received)

    mixed_far = mix(keep_far, received_far)
    blocks = tuple(mix(keep_near, received_near)) + tuple(mixed_far)

    moved = []
    for index in range(count):
        e, dy, dx = index // 4, index // 2 % 2, index % 2
        mapping = lambda z, c, y, x, e=e, dy=dy, dx=dx: (2 * (z // 2 ^ e) + c, x, y ^ dy, z % 2 ^ dx)
        moved.append(hop(blocks[index], mapping))
    gram = pl.pallas_call(
        gram_kernel,
        out_shape=f32(16, 128),
        in_specs=[SM] + [VM] * count,
        out_specs=VM,
        compiler_params=pltpu.CompilerParams(vmem_limit_bytes=SHARED),
        name="gram",
    )(place, *moved)
    along = [hop(gram, lambda z, c, y, x, d=d: (z ^ d, c, y, x)) for d in range(1, z_count)]
    gram = plane_sum((gram + along[0]) + (along[1] + along[2]))
    out = pl.pallas_call(
        place_kernel,
        out_shape=f32(HALF, 4 * part),
        in_specs=[SM] + [VM] * (4 + count),
        out_specs=VM,
        scratch_shapes=[pltpu.VMEM((2 * part // HALF, 2, HALF, HALF), jnp.float32)],
        compiler_params=pltpu.CompilerParams(vmem_limit_bytes=SHARED),
        name="place",
    )(place, *gram, *moved)
    return out.T


def exchange(own, other):
    along_x = hop(other, lambda z, c, y, x: (z, c, y, 1 - x))
    across = hop(other, lambda z, c, y, x: (z, c, 1 - y, 1 - x))
    along_y = hop(own, lambda z, c, y, x: (z, c, 1 - y, x))
    return own, along_x, along_y, across


def plane_sum(value):
    value = value + hop(value, lambda z, c, y, x: (z, 1 - c, y, x))
    across = [hop(value, lambda z, c, y, x, d=d: (z, c, y ^ (d >> 1), x ^ (d & 1))) for d in (1, 2, 3)]
    return [value] + across


def fits(images, mesh):
    return (
        mesh.shape["local"] == 4
        and mesh.shape["node"] == 8
        and images.shape[3] == mesh.shape["node"] * HALF
        and images.shape[0] // mesh.size == 8
    )


def solution(mesh):
    def run(images, targets, weight):
        tiled = fits(images, mesh)
        step = jax.shard_map(
            tile_plan if tiled else general_plan,
            mesh=mesh,
            in_specs=(
                P(("node", "local"), None, None, None),
                P(("node", "local"), None, None, None),
                P(),
            ),
            out_specs=P("local", "node"),
            check_vma=False,
        )
        return step(images, targets, weight)

    return run
```

```python
import jax
import jax.numpy as jnp
from jax import lax
from jax.experimental import pallas as pl
from jax.experimental.pallas import tpu as pltpu
from jax.sharding import PartitionSpec as P


epsilon = 1e-06
HALF = 64
BLK = 32
AHEAD = 2
SHARED = 24 * 2**20
ALONE = 65 * 2**20


def partner(value, axis, distance):
    mask = 2**distance
    pairs = [(source, source ^ mask) for source in range(lax.axis_size(axis))]
    return lax.ppermute(value, axis, pairs)


def make_patches(images):
    side = images.shape[1]
    padded = jnp.pad(images, ((0, 0), (1, 1), (1, 1), (0, 0)))
    tap_views = []
    for row_shift in range(3):
        for col_shift in range(3):
            tap_views.append(padded[:, row_shift : row_shift + side, col_shift : col_shift + side, :])
    joined = jnp.concatenate(tap_views, axis=-1)
    return joined.reshape(-1, 9 * images.shape[3])


def adasum_pair(left_vec, right_vec, cross_sum, left_sq, right_sq):
    left_coef = 1.0 - cross_sum / (2.0 * (left_sq + epsilon))
    right_coef = 1.0 - cross_sum / (2.0 * (right_sq + epsilon))
    return left_coef * left_vec + right_coef * right_vec


def general_plan(images, targets, weight):
    channels = images.shape[3]
    flat_w = weight.reshape(9 * channels, channels)
    patches = make_patches(images)
    outputs = jnp.dot(patches, flat_w, precision=lax.Precision.HIGHEST, preferred_element_type=jnp.float32)
    residual = outputs - targets.reshape(-1, channels)
    row_scale = 1.0 / patches.shape[0]
    product = lax.dot_general(
        patches,
        residual,
        (((0,), (0,)), ((), ())),
        precision=lax.Precision.HIGHEST,
        preferred_element_type=jnp.float32,
    )
    my_rows = lax.psum_scatter(product * row_scale, "local", scatter_dimension=0, tiled=True)
    node_count = lax.axis_size("node")
    levels = node_count.bit_length() - 1
    row_count = my_rows.shape[0]
    col_width = channels // node_count
    node_id = lax.axis_index("node")
    piece_blocks = my_rows.reshape(row_count, node_count, col_width)
    for tree_level in range(levels):
        is_upper = jnp.bitwise_and(jnp.right_shift(node_id, tree_level), 1) == 1
        remaining = piece_blocks.shape[1]
        split_view = piece_blocks.reshape(row_count, remaining // 2, 2, col_width)
        lower_half = split_view[:, :, 0, :]
        upper_half = split_view[:, :, 1, :]
        kept_part = jnp.where(is_upper, upper_half, lower_half)
        sent_part = jnp.where(is_upper, lower_half, upper_half)
        received = partner(sent_part, "node", tree_level)
        first_part = jnp.where(is_upper, received, kept_part)
        second_part = jnp.where(is_upper, kept_part, received)
        totals = jnp.stack(
            [
                jnp.sum(first_part * second_part),
                jnp.sum(first_part * first_part),
                jnp.sum(second_part * second_part),
            ]
        )
        totals = lax.psum(totals, "local")
        for inner_bit in range(tree_level + 1):
            totals = totals + partner(totals, "node", inner_bit)
        piece_blocks = adasum_pair(first_part, second_part, totals[0], totals[1], totals[2])
    return piece_blocks.reshape(row_count, col_width)


def hop(value, mapping):
    z_count = lax.axis_size("node") // 2
    pairs = []
    for z in range(z_count):
        for c in range(2):
            for y in range(2):
                for x in range(2):
                    tz, tc, ty, tx = mapping(z, c, y, x)
                    pairs.append((((z * 2 + c) * 2 + y) * 2 + x, ((tz * 2 + tc) * 2 + ty) * 2 + tx))
    return lax.ppermute(value, ("node", "local"), pairs)


def split2(v):
    hi = v.astype(jnp.bfloat16)
    lo = (v - hi.astype(jnp.float32)).astype(jnp.bfloat16)
    return hi, lo


def mm(a, b):
    return jnp.dot(a, b, preferred_element_type=jnp.float32)


def low_lanes(shape):
    return lax.broadcasted_iota(jnp.int32, shape, len(shape) - 1) < HALF


def pair_pack(a, b):
    low = low_lanes(a.shape)
    axis = a.ndim - 1
    return (jnp.where(low, a, pltpu.roll(b, HALF, axis)), jnp.where(low, pltpu.roll(a, HALF, axis), b))


def lane_halves(v):
    evens, odds = [], []
    for k in range(v.shape[1] // 256):
        e, o = pair_pack(v[:, 256 * k : 256 * k + 128], v[:, 256 * k + 128 : 256 * k + 256])
        evens.append(e)
        odds.append(o)
    return jnp.concatenate(evens, axis=1), jnp.concatenate(odds, axis=1)


def split_kernel(s_ref, x_ref, own_ref, other_ref, buf, halves, in_sems, out_sems):
    strips, strip, _ = buf.shape
    spans = [pl.ds(r * strip, strip) for r in range(strips)]
    copies = fetch([x_ref.at[span] for span in spans], [buf.at[r] for r in range(strips)], in_sems)
    up = s_ref[0] == 1
    stores = []
    for r in range(strips):
        copies[r].wait()
        even, odd = lane_halves(buf[r])
        halves[2 * r] = jnp.where(up, odd, even)
        halves[2 * r + 1] = jnp.where(up, even, odd)
        for k, ref in enumerate((own_ref, other_ref)):
            stores.append(pltpu.make_async_copy(halves.at[2 * r + k], ref.at[spans[r]], out_sems.at[2 * r + k]))
            stores[-1].start()
    for store in stores:
        store.wait()


def residual_kernel(s_ref, x_ref, t_ref, w_ref, own_far, other_far, own_near, other_near, *scratch):
    x_buf, t_buf, w_buf, left_ref, acc_ref, sems, w_sems = scratch
    side = acc_ref.shape[0] - 2
    imgs, cols = acc_ref.shape[2:]
    taps = w_buf.shape[0]
    (x_copy,) = fetch([x_ref], [x_buf], sems)
    fetch([w_ref.at[tap] for tap in range(AHEAD)], [w_buf.at[tap] for tap in range(AHEAD)], w_sems)
    acc_ref[...] = jnp.zeros(acc_ref.shape, jnp.float32)
    x_copy.wait()
    xh, xl = split2(x_buf[...])
    left_ref[...] = jnp.concatenate([xh, xh, xl], axis=1)
    t_copy = pltpu.make_async_copy(t_ref, t_buf, sems.at[1])
    t_copy.start()

    def add_tap(tap, carry):
        pltpu.make_async_copy(w_ref.at[tap], w_buf.at[tap], w_sems.at[tap]).wait()

        @pl.when(tap + AHEAD < taps)
        def _():
            later = tap + AHEAD
            pltpu.make_async_copy(w_ref.at[later], w_buf.at[later], w_sems.at[later]).start()

        wh, wl = split2(w_buf[tap])
        product = mm(left_ref[...], jnp.concatenate([wh, wl, wh], axis=0))
        at = (pl.ds(2 - tap // 3, side), pl.ds(2 - tap % 3, side))
        acc_ref[at] += product.reshape(side, side, imgs, cols)
        return carry

    lax.fori_loop(0, taps, add_tap, 0)
    t_copy.wait()
    total = acc_ref[1 : side + 1, 1 : side + 1].reshape(t_buf.shape) - t_buf[...]
    even, odd = lane_halves(total)
    up, high = s_ref[0] == 1, s_ref[1] == 1
    own, other = jnp.where(up, odd, even), jnp.where(up, even, odd)
    for value, near, far in ((own, own_near, own_far), (other, other_near, other_far)):
        near[...] = jnp.where(high, value[:, 128:], value[:, :128])
        far[...] = jnp.where(high, value[:, :128], value[:, 128:])


def prepare_kernel(side, *refs):
    sources, (out_ref, buf, sems) = refs[:4], refs[4:]
    copies = fetch(sources, [buf.at[i] for i in range(4)], sems)
    _, _, width = buf.shape
    span = out_ref.shape[2] // 2
    for copy in copies:
        copy.wait()
    for r in range(side):
        strip = gather([buf.at[i] for i in range(4)], r, side)
        strip = strip.reshape(-1, width)
        strip = jnp.concatenate([strip, jnp.zeros((span - strip.shape[0], width), jnp.float32)], axis=0)
        xh, xl = split2(strip.T)
        out_ref[r, :, :span] = xh
        out_ref[r, :, span:] = xl


def gather(refs, r, side):
    strip = refs[0].shape[0] // side
    parts = [ref[r * strip : (r + 1) * strip, :].reshape(side, strip // side, -1) for ref in refs]
    return jnp.concatenate(parts, axis=1)


def gradient_kernel(scale, side, s_ref, xt_ref, *refs):
    sources, outs, (rh, rl, g_ref) = refs[:4], refs[4:-3], refs[-3:]
    keep_ref, send_ref = outs[:2]
    xt = xt_ref
    width = sources[0].shape[1]
    span = xt.shape[2] // 2
    for ref in (rh, rl):
        for edge in (0, side + 1, side + 2):
            ref[:, edge] = jnp.zeros((side,) + ref.shape[2:], jnp.bfloat16)
    for r in range(side):
        h, lo = split2(gather(sources, r, side))
        rh[r, 1 : side + 1] = h
        rl[r, 1 : side + 1] = lo
    totals = [None] * 9
    for r in range(side):
        taps = [(i, j) for i in range(3) for j in range(3) if 0 <= r - i + 1 < side]

        def strips(ref):
            return [ref[r - i + 1, 2 - j : 2 - j + side + 1].reshape(span, width) for i, j in taps]

        bh, bl = jnp.concatenate(strips(rh), axis=1), jnp.concatenate(strips(rl), axis=1)
        xh, xl = xt[r, :, :span], xt[r, :, span:]
        product = mm(jnp.concatenate([xh, xh, xl], axis=1), jnp.concatenate([bh, bl, bh], axis=0))
        for n, (i, j) in enumerate(taps):
            piece = product[:, n * width : (n + 1) * width]
            tap = 3 * i + j
            totals[tap] = piece if totals[tap] is None else totals[tap] + piece
    blocks = g_ref.shape[0] // 9
    for tap in range(9):
        g_ref[tap * blocks : (tap + 1) * blocks] = (totals[tap] * scale).reshape(blocks, BLK, width)
    odd = s_ref[0] == 1
    per = g_ref.shape[0] // 8
    for quarter in range(4):
        slot = 2 * jnp.bitwise_xor(quarter // 2, s_ref[1]) + jnp.bitwise_xor(quarter % 2, s_ref[2])
        for m in range(per):
            first, second = pair_pack(g_ref[2 * per * quarter + m], g_ref[2 * per * quarter + per + m])
            keep_ref[slot, m * BLK : (m + 1) * BLK, :] = jnp.where(odd, second, first)
            send_ref[slot, m * BLK : (m + 1) * BLK, :] = jnp.where(odd, first, second)
    for early, ref in zip(outs[2:], outs[:2]):
        early[...] = ref[ref.shape[0] - 1]


def column_sums(a, b):
    return jnp.sum((a * b).reshape(-1, a.shape[-1]), axis=0, keepdims=True)


def fetch(sources, slots, sems):
    copies = [pltpu.make_async_copy(src, dst, sems.at[i]) for i, (src, dst) in enumerate(zip(sources, slots))]
    for copy in copies:
        copy.start()
    return copies


def pair_dots_kernel(s_ref, keep_ref, received_ref, *refs):
    core = s_ref[0]
    out_ref = refs[-1]
    cross = mine = theirs = jnp.zeros((1, out_ref.shape[1]), jnp.float32)
    for d in range(keep_ref.shape[0]):
        a, b = keep_ref[d], received_ref[d]
        cross += column_sums(a, b)
        mine += column_sums(a, a)
        theirs += column_sums(b, b)
    left, right = jnp.where(core == 0, mine, theirs), jnp.where(core == 0, theirs, mine)
    if len(refs) > 1:
        before = refs[0]
        cross, left, right = cross + before[0:1], left + before[1:2], right + before[2:3]
    out_ref[...] = jnp.zeros(out_ref.shape, jnp.float32)
    out_ref[0:1] = cross
    out_ref[1:2] = left
    out_ref[2:3] = right


def pair_coefs(cross, left_sq, right_sq):
    return 1.0 - cross / (2.0 * (left_sq + epsilon)), 1.0 - cross / (2.0 * (right_sq + epsilon))


def sum_four(refs):
    return (refs[0][...] + refs[1][...]) + (refs[2][...] + refs[3][...])


def pair_mix_kernel(pieces, s_ref, t0, t1, t2, t3, keep_ref, received_ref, *out_refs):
    core = s_ref[0]
    totals = jnp.sum(sum_four((t0, t1, t2, t3)), axis=1, keepdims=True)
    left, right = pair_coefs(totals[0:1], totals[1:2], totals[2:3])
    keep_coef = jnp.where(core == 0, left, right)
    received_coef = jnp.where(core == 0, right, left)
    for d, out in enumerate(out_refs[:pieces]):
        out[...] = keep_coef * keep_ref[d] + received_coef * received_ref[d]
    for out in out_refs[pieces:]:
        out[...] = jnp.zeros(out.shape, jnp.float32)
        out[0:1] = jnp.broadcast_to(keep_coef, (1, out.shape[1]))
        out[1:2] = jnp.broadcast_to(received_coef, (1, out.shape[1]))


def gram_kernel(s_ref, *refs):
    upper, x = s_ref[0], s_ref[1]
    coefs, own, other, gram_ref, late_ref = refs[7:]
    late_ref[...] = coefs[0:1] * own[...] + coefs[1:2] * other[...]
    blocks = refs[:7] + (late_ref,)
    node = [2 * jnp.bitwise_xor(upper, d // 2) + jnp.bitwise_xor(x, d % 2) for d in range(4)]
    for e in range(4):
        for d in range(e + 1):
            value = sum(column_sums(blocks[slot_of(d, dy)][...], blocks[slot_of(e, dy)][...]) for dy in range(2))
            gram_ref[pl.ds(4 * node[d] + node[e], 1)] = value
            gram_ref[pl.ds(4 * node[e] + node[d], 1)] = value


def slot_of(d, dy):
    return 4 * (d // 2) + 2 * dy + d % 2


def place_kernel(s_ref, *refs):
    upper, x, y = s_ref[0], s_ref[1], s_ref[2]
    blocks, (out_ref, rows_ref) = refs[4:12], refs[12:]
    gram = jnp.sum(sum_four(refs[:4]), axis=1, keepdims=True)
    g = lambda a, b: gram[4 * a + b : 4 * a + b + 1]
    p = pair_coefs(g(0, 1), g(0, 0), g(1, 1)) + pair_coefs(g(2, 3), g(2, 2), g(3, 3))
    cross = p[0] * (p[2] * g(0, 2) + p[3] * g(0, 3)) + p[1] * (p[2] * g(1, 2) + p[3] * g(1, 3))
    near = p[0] * p[0] * g(0, 0) + 2.0 * p[0] * p[1] * g(0, 1) + p[1] * p[1] * g(1, 1)
    far = p[2] * p[2] * g(2, 2) + 2.0 * p[2] * p[3] * g(2, 3) + p[3] * p[3] * g(3, 3)
    near_coef, far_coef = pair_coefs(cross, near, far)
    absolute = (near_coef * p[0], near_coef * p[1], far_coef * p[2], far_coef * p[3])
    coefs = []
    for d in range(4):
        owner = 2 * jnp.bitwise_xor(upper, d // 2) + jnp.bitwise_xor(x, d % 2)
        coef = absolute[3]
        for a in range(3):
            coef = jnp.where(owner == a, absolute[a], coef)
        coefs.append(coef)
    for dy in range(2):
        part = [blocks[slot_of(d, dy)][...] for d in range(4)]
        block = coefs[0] * part[0] + coefs[1] * part[1] + (coefs[2] * part[2] + coefs[3] * part[3])
        upper_half = pltpu.roll(block, HALF, 1)
        rows = jnp.concatenate([block[:, :HALF], upper_half[:, :HALF]], axis=0)
        rows = rows.reshape(rows_ref.shape[0], HALF, HALF)
        slot = jnp.bitwise_xor(y, dy)
        for k in range(rows_ref.shape[0]):
            rows_ref[k, slot] = rows[k]
    out_ref[...] = rows_ref[...].reshape(out_ref.shape[1], HALF).T


VM = pl.BlockSpec(memory_space=pltpu.VMEM)
HB = pl.BlockSpec(memory_space=pltpu.HBM)
SM = pl.BlockSpec(memory_space=pltpu.SMEM)


def f32(*shape):
    return jax.ShapeDtypeStruct(shape, jnp.float32)


def tile_plan(images, targets, weight):
    return tiles(images, targets, weight)


def tiles(images, targets, weight):
    imgs, side, _, channels = images.shape
    width = channels // 2
    rows = side * side * imgs
    node_id = lax.axis_index("node")
    local_id = lax.axis_index("local")
    z, c = node_id // 2, node_id % 2
    y, x = local_id // 2, local_id % 2

    def scalars(*values):
        return jnp.stack([jnp.asarray(v, jnp.int32) for v in values])

    xt = jnp.transpose(images, (1, 2, 0, 3))
    x_own, x_other = pl.pallas_call(
        split_kernel,
        out_shape=(f32(rows, width), f32(rows, width)),
        in_specs=[SM, HB],
        out_specs=(HB, HB),
        scratch_shapes=[
            pltpu.VMEM((side, rows // side, channels), jnp.float32),
            pltpu.VMEM((2 * side, rows // side, width), jnp.float32),
            pltpu.SemaphoreType.DMA((side,)),
            pltpu.SemaphoreType.DMA((2 * side,)),
        ],
        compiler_params=pltpu.CompilerParams(vmem_limit_bytes=ALONE),
        name="split_images",
    )(scalars(y), xt.reshape(rows, channels))
    x_y = hop(x_other, lambda z, c, y, x: (z, c, 1 - y, x))
    x_x = hop(x_own, lambda z, c, y, x: (z, c, y, 1 - x))
    x_d = hop(x_other, lambda z, c, y, x: (z, c, 1 - y, 1 - x))

    tt = jnp.transpose(targets, (1, 2, 0, 3)).reshape(rows, channels)
    taps = weight.shape[0] * weight.shape[1]
    own_far, other_far, own_near, other_near = pl.pallas_call(
        residual_kernel,
        out_shape=(f32(rows, 128),) * 4,
        in_specs=[SM] + [HB] * 3,
        out_specs=(VM,) * 4,
        scratch_shapes=[
            pltpu.VMEM((rows, channels), jnp.float32),
            pltpu.VMEM((rows, channels), jnp.float32),
            pltpu.VMEM((taps, channels, channels), jnp.float32),
            pltpu.VMEM((rows, 3 * channels), jnp.bfloat16),
            pltpu.VMEM((side + 2, side + 2, imgs, channels), jnp.float32),
            pltpu.SemaphoreType.DMA((2,)),
            pltpu.SemaphoreType.DMA((taps,)),
        ],
        cost_estimate=pl.CostEstimate(
            flops=6 * rows * taps * channels * channels, bytes_accessed=4 * taps * channels * channels, transcendentals=0
        ),
        compiler_params=pltpu.CompilerParams(vmem_limit_bytes=ALONE),
        name="residual",
    )(scalars(x, z // 2), xt.reshape(rows, channels), tt, weight.reshape(taps, channels, channels))
    far = exchange(own_far, other_far)
    near = exchange(own_near, other_near)

    span = (side + 1) * 4 * imgs
    xt_shape = (side, width, 2 * span)
    images_t = pl.pallas_call(
        lambda *refs: prepare_kernel(side, *refs),
        out_shape=jax.ShapeDtypeStruct(xt_shape, jnp.bfloat16),
        in_specs=[HB] * 4,
        out_specs=VM,
        scratch_shapes=[pltpu.VMEM((4, rows, width), jnp.float32), pltpu.SemaphoreType.DMA((4,))],
        compiler_params=pltpu.CompilerParams(vmem_limit_bytes=SHARED),
        name="prepare",
    )(x_own, x_x, x_y, x_d)

    z_count = lax.axis_size("node") // 2
    part = taps * width // 8
    count = 2 * z_count
    half = count // 2
    place = scalars(z // 2, x, y)

    def gradient(pieces, early):
        return pl.pallas_call(
            lambda *refs: gradient_kernel(1.0 / rows, side, *refs),
            out_shape=(f32(half, part, 128),) * 2 + (f32(part, 128),) * early,
            in_specs=[SM] + [VM] * 5,
            out_specs=(VM,) * (2 + early),
            scratch_shapes=[
                pltpu.VMEM((side, side + 3, 4 * imgs, 128), jnp.bfloat16),
                pltpu.VMEM((side, side + 3, 4 * imgs, 128), jnp.bfloat16),
                pltpu.VMEM((taps * width // BLK, BLK, 128), jnp.float32),
            ],
            cost_estimate=pl.CostEstimate(
                flops=24 * rows * taps * width * 128, bytes_accessed=4 * taps * width * 128, transcendentals=0
            ),
            compiler_params=pltpu.CompilerParams(vmem_limit_bytes=SHARED),
        )(scalars(c, y, z % 2), images_t, *pieces)

    def dots(keep, received, before):
        return pl.pallas_call(
            pair_dots_kernel,
            out_shape=f32(8, 128),
            in_specs=[SM, VM, VM] + [VM] * len(before),
            out_specs=VM,
            compiler_params=pltpu.CompilerParams(vmem_limit_bytes=SHARED),
        )(scalars(c), keep, received, *before)

    across = lambda z, c, y, x: (z, 1 - c, y, x)
    keep_far, send_far, early_keep, early_send = gradient(far, 2)
    received_far = hop(send_far, across)
    last = half - 1
    early_own = hop(early_keep, mover(count - 1))
    early_other = hop(early_send, lambda z, c, y, x: mover(count - 1)(z, 1 - c, y, x))
    keep_near, send_near = gradient(near, 0)
    received_near = hop(send_near, across)
    totals = dots(keep_far, received_far, ())
    totals = plane_sum(dots(keep_near, received_near, (totals,)))

    def mix(keep, received, pieces):
        return pl.pallas_call(
            lambda *refs: pair_mix_kernel(pieces, *refs),
            out_shape=(f32(part, 128),) * pieces + (f32(8, 128),) * (half - pieces),
            in_specs=[SM] + [VM] * 6,
            out_specs=(VM,) * half,
            compiler_params=pltpu.CompilerParams(vmem_limit_bytes=SHARED),
        )(scalars(c), *totals, keep, received)

    mixed_far = mix(keep_far, received_far, last)
    blocks = tuple(mix(keep_near, received_near, half)) + tuple(mixed_far)

    moved = [hop(blocks[index], mover(index)) for index in range(count)]
    gram, moved[-1] = pl.pallas_call(
        gram_kernel,
        out_shape=(f32(16, 128), f32(part, 128)),
        in_specs=[SM] + [VM] * (count + 2),
        out_specs=(VM, VM),
        compiler_params=pltpu.CompilerParams(vmem_limit_bytes=SHARED),
        name="gram",
    )(place, *moved, early_own, early_other)
    along = [hop(gram, lambda z, c, y, x, d=d: (z ^ d, c, y, x)) for d in range(1, z_count)]
    gram = plane_sum((gram + along[0]) + (along[1] + along[2]))
    out = pl.pallas_call(
        place_kernel,
        out_shape=f32(HALF, 4 * part),
        in_specs=[SM] + [VM] * (4 + count),
        out_specs=VM,
        scratch_shapes=[pltpu.VMEM((2 * part // HALF, 2, HALF, HALF), jnp.float32)],
        compiler_params=pltpu.CompilerParams(vmem_limit_bytes=SHARED),
        name="place",
    )(place, *gram, *moved)
    return out.T


def mover(index):
    e, dy, dx = index // 4, index // 2 % 2, index % 2
    return lambda z, c, y, x: (2 * (z // 2 ^ e) + c, x, y ^ dy, z % 2 ^ dx)


def exchange(own, other):
    along_x = hop(other, lambda z, c, y, x: (z, c, y, 1 - x))
    across = hop(other, lambda z, c, y, x: (z, c, 1 - y, 1 - x))
    along_y = hop(own, lambda z, c, y, x: (z, c, 1 - y, x))
    return own, along_x, along_y, across


def plane_sum(value):
    value = value + hop(value, lambda z, c, y, x: (z, 1 - c, y, x))
    across = [hop(value, lambda z, c, y, x, d=d: (z, c, y ^ (d >> 1), x ^ (d & 1))) for d in (1, 2, 3)]
    return [value] + across


def fits(images, mesh):
    return (
        mesh.shape["local"] == 4
        and mesh.shape["node"] == 8
        and images.shape[3] == mesh.shape["node"] * HALF
        and images.shape[0] // mesh.size == 8
    )


def solution(mesh):
    def run(images, targets, weight):
        tiled = fits(images, mesh)
        step = jax.shard_map(
            tile_plan if tiled else general_plan,
            mesh=mesh,
            in_specs=(
                P(("node", "local"), None, None, None),
                P(("node", "local"), None, None, None),
                P(),
            ),
            out_specs=P("local", "node"),
            check_vma=False,
        )
        return step(images, targets, weight)

    return run
```

```python
import jax
import jax.numpy as jnp
from jax import lax
from jax.experimental import pallas as pl
from jax.experimental.pallas import tpu as pltpu
from jax.sharding import PartitionSpec as P


epsilon = 1e-06
HALF = 64
BLK = 32
AHEAD = 2
SHARED = 24 * 2**20
ALONE = 58 * 2**20


def partner(value, axis, distance):
    mask = 2**distance
    pairs = [(source, source ^ mask) for source in range(lax.axis_size(axis))]
    return lax.ppermute(value, axis, pairs)


def make_patches(images):
    side = images.shape[1]
    padded = jnp.pad(images, ((0, 0), (1, 1), (1, 1), (0, 0)))
    tap_views = []
    for row_shift in range(3):
        for col_shift in range(3):
            tap_views.append(padded[:, row_shift : row_shift + side, col_shift : col_shift + side, :])
    joined = jnp.concatenate(tap_views, axis=-1)
    return joined.reshape(-1, 9 * images.shape[3])


def adasum_pair(left_vec, right_vec, cross_sum, left_sq, right_sq):
    left_coef = 1.0 - cross_sum / (2.0 * (left_sq + epsilon))
    right_coef = 1.0 - cross_sum / (2.0 * (right_sq + epsilon))
    return left_coef * left_vec + right_coef * right_vec


def general_plan(images, targets, weight):
    channels = images.shape[3]
    flat_w = weight.reshape(9 * channels, channels)
    patches = make_patches(images)
    outputs = jnp.dot(patches, flat_w, precision=lax.Precision.HIGHEST, preferred_element_type=jnp.float32)
    residual = outputs - targets.reshape(-1, channels)
    row_scale = 1.0 / patches.shape[0]
    product = lax.dot_general(
        patches,
        residual,
        (((0,), (0,)), ((), ())),
        precision=lax.Precision.HIGHEST,
        preferred_element_type=jnp.float32,
    )
    my_rows = lax.psum_scatter(product * row_scale, "local", scatter_dimension=0, tiled=True)
    node_count = lax.axis_size("node")
    levels = node_count.bit_length() - 1
    row_count = my_rows.shape[0]
    col_width = channels // node_count
    node_id = lax.axis_index("node")
    piece_blocks = my_rows.reshape(row_count, node_count, col_width)
    for tree_level in range(levels):
        is_upper = jnp.bitwise_and(jnp.right_shift(node_id, tree_level), 1) == 1
        remaining = piece_blocks.shape[1]
        split_view = piece_blocks.reshape(row_count, remaining // 2, 2, col_width)
        lower_half = split_view[:, :, 0, :]
        upper_half = split_view[:, :, 1, :]
        kept_part = jnp.where(is_upper, upper_half, lower_half)
        sent_part = jnp.where(is_upper, lower_half, upper_half)
        received = partner(sent_part, "node", tree_level)
        first_part = jnp.where(is_upper, received, kept_part)
        second_part = jnp.where(is_upper, kept_part, received)
        totals = jnp.stack(
            [
                jnp.sum(first_part * second_part),
                jnp.sum(first_part * first_part),
                jnp.sum(second_part * second_part),
            ]
        )
        totals = lax.psum(totals, "local")
        for inner_bit in range(tree_level + 1):
            totals = totals + partner(totals, "node", inner_bit)
        piece_blocks = adasum_pair(first_part, second_part, totals[0], totals[1], totals[2])
    return piece_blocks.reshape(row_count, col_width)


def hop(value, mapping):
    z_count = lax.axis_size("node") // 2
    pairs = []
    for z in range(z_count):
        for c in range(2):
            for y in range(2):
                for x in range(2):
                    tz, tc, ty, tx = mapping(z, c, y, x)
                    pairs.append((((z * 2 + c) * 2 + y) * 2 + x, ((tz * 2 + tc) * 2 + ty) * 2 + tx))
    return lax.ppermute(value, ("node", "local"), pairs)


def split2(v):
    hi = v.astype(jnp.bfloat16)
    lo = (v - hi.astype(jnp.float32)).astype(jnp.bfloat16)
    return hi, lo


def mm(a, b):
    return jnp.dot(a, b, preferred_element_type=jnp.float32)


def low_lanes(shape):
    return lax.broadcasted_iota(jnp.int32, shape, len(shape) - 1) < HALF


def pair_pack(a, b):
    low = low_lanes(a.shape)
    axis = a.ndim - 1
    return (jnp.where(low, a, pltpu.roll(b, HALF, axis)), jnp.where(low, pltpu.roll(a, HALF, axis), b))


def lane_halves(v):
    evens, odds = [], []
    for k in range(v.shape[1] // 256):
        e, o = pair_pack(v[:, 256 * k : 256 * k + 128], v[:, 256 * k + 128 : 256 * k + 256])
        evens.append(e)
        odds.append(o)
    return jnp.concatenate(evens, axis=1), jnp.concatenate(odds, axis=1)


def split_kernel(s_ref, x_ref, own_ref, other_ref, buf, sems):
    strips, strip, _ = buf.shape
    spans = [pl.ds(r * strip, strip) for r in range(strips)]
    copies = fetch([x_ref.at[span] for span in spans], [buf.at[r] for r in range(strips)], sems)
    up = s_ref[0] == 1
    for r in range(strips):
        copies[r].wait()
        even, odd = lane_halves(buf[r])
        own_ref[spans[r]] = jnp.where(up, odd, even)
        other_ref[spans[r]] = jnp.where(up, even, odd)


def residual_kernel(s_ref, x_ref, t_ref, w_ref, own_far, other_far, own_near, other_near, *scratch):
    x_buf, t_buf, w_buf, left_ref, acc_ref, sems, w_sems = scratch
    side = acc_ref.shape[0] - 2
    imgs, cols = acc_ref.shape[2:]
    taps = w_buf.shape[0]
    (x_copy,) = fetch([x_ref], [x_buf], sems)
    fetch([w_ref.at[tap] for tap in range(AHEAD)], [w_buf.at[tap] for tap in range(AHEAD)], w_sems)
    acc_ref[...] = jnp.zeros(acc_ref.shape, jnp.float32)
    x_copy.wait()
    xh, xl = split2(x_buf[...])
    left_ref[...] = jnp.concatenate([xh, xh, xl], axis=1)
    t_copy = pltpu.make_async_copy(t_ref, t_buf, sems.at[1])
    t_copy.start()

    def add_tap(tap, carry):
        pltpu.make_async_copy(w_ref.at[tap], w_buf.at[tap], w_sems.at[tap]).wait()

        @pl.when(tap + AHEAD < taps)
        def _():
            later = tap + AHEAD
            pltpu.make_async_copy(w_ref.at[later], w_buf.at[later], w_sems.at[later]).start()

        wh, wl = split2(w_buf[tap])
        product = mm(left_ref[...], jnp.concatenate([wh, wl, wh], axis=0))
        at = (pl.ds(2 - tap // 3, side), pl.ds(2 - tap % 3, side))
        acc_ref[at] += product.reshape(side, side, imgs, cols)
        return carry

    lax.fori_loop(0, taps, add_tap, 0)
    t_copy.wait()
    total = acc_ref[1 : side + 1, 1 : side + 1].reshape(t_buf.shape) - t_buf[...]
    even, odd = lane_halves(total)
    up, high = s_ref[0] == 1, s_ref[1] == 1
    own, other = jnp.where(up, odd, even), jnp.where(up, even, odd)
    for value, near, far in ((own, own_near, own_far), (other, other_near, other_far)):
        near[...] = jnp.where(high, value[:, 128:], value[:, :128])
        far[...] = jnp.where(high, value[:, :128], value[:, 128:])


def prepare_kernel(side, *refs):
    sources, (far_ref, near_ref, out_ref, far_out, near_out) = refs[:4], refs[4:]
    far_out[...] = far_ref[...]
    near_out[...] = near_ref[...]
    width = sources[0].shape[1]
    span = out_ref.shape[2] // 2
    for r in range(side):
        strip = gather(sources, r, side)
        strip = strip.reshape(-1, width)
        strip = jnp.concatenate([strip, jnp.zeros((span - strip.shape[0], width), jnp.float32)], axis=0)
        xh, xl = split2(strip.T)
        out_ref[r, :, :span] = xh
        out_ref[r, :, span:] = xl


def gather(refs, r, side):
    strip = refs[0].shape[0] // side
    parts = [ref[r * strip : (r + 1) * strip, :].reshape(side, strip // side, -1) for ref in refs]
    return jnp.concatenate(parts, axis=1)


def gradient_kernel(scale, side, s_ref, xt_ref, *refs):
    sources, outs, (rh, rl, g_ref) = refs[:4], refs[4:-3], refs[-3:]
    keep_ref, send_ref = outs[:2]
    xt = xt_ref
    width = sources[0].shape[1]
    span = xt.shape[2] // 2
    for ref in (rh, rl):
        for edge in (0, side + 1, side + 2):
            ref[:, edge] = jnp.zeros((side,) + ref.shape[2:], jnp.bfloat16)
    for r in range(side):
        h, lo = split2(gather(sources, r, side))
        rh[r, 1 : side + 1] = h
        rl[r, 1 : side + 1] = lo
    totals = [None] * 9
    for r in range(side):
        taps = [(i, j) for i in range(3) for j in range(3) if 0 <= r - i + 1 < side]

        def strips(ref):
            return [ref[r - i + 1, 2 - j : 2 - j + side + 1].reshape(span, width) for i, j in taps]

        bh, bl = jnp.concatenate(strips(rh), axis=1), jnp.concatenate(strips(rl), axis=1)
        xh, xl = xt[r, :, :span], xt[r, :, span:]
        product = mm(jnp.concatenate([xh, xh, xl], axis=1), jnp.concatenate([bh, bl, bh], axis=0))
        for n, (i, j) in enumerate(taps):
            piece = product[:, n * width : (n + 1) * width]
            tap = 3 * i + j
            totals[tap] = piece if totals[tap] is None else totals[tap] + piece
    blocks = g_ref.shape[0] // 9
    for tap in range(9):
        g_ref[tap * blocks : (tap + 1) * blocks] = (totals[tap] * scale).reshape(blocks, BLK, width)
    odd = s_ref[0] == 1
    per = g_ref.shape[0] // 8
    for quarter in range(4):
        slot = 2 * jnp.bitwise_xor(quarter // 2, s_ref[1]) + jnp.bitwise_xor(quarter % 2, s_ref[2])
        for m in range(per):
            first, second = pair_pack(g_ref[2 * per * quarter + m], g_ref[2 * per * quarter + per + m])
            keep_ref[slot, m * BLK : (m + 1) * BLK, :] = jnp.where(odd, second, first)
            send_ref[slot, m * BLK : (m + 1) * BLK, :] = jnp.where(odd, first, second)
    for early, ref in zip(outs[2:], outs[:2]):
        early[...] = ref[ref.shape[0] - 1]


def column_sums(a, b):
    return jnp.sum((a * b).reshape(-1, a.shape[-1]), axis=0, keepdims=True)


def fetch(sources, slots, sems):
    copies = [pltpu.make_async_copy(src, dst, sems.at[i]) for i, (src, dst) in enumerate(zip(sources, slots))]
    for copy in copies:
        copy.start()
    return copies


def pair_dots_kernel(s_ref, keep_ref, received_ref, *refs):
    core = s_ref[0]
    out_ref = refs[-1]
    cross = mine = theirs = jnp.zeros((1, out_ref.shape[1]), jnp.float32)
    for d in range(keep_ref.shape[0]):
        a, b = keep_ref[d], received_ref[d]
        cross += column_sums(a, b)
        mine += column_sums(a, a)
        theirs += column_sums(b, b)
    left, right = jnp.where(core == 0, mine, theirs), jnp.where(core == 0, theirs, mine)
    if len(refs) > 1:
        before = refs[0]
        cross, left, right = cross + before[0:1], left + before[1:2], right + before[2:3]
    out_ref[...] = jnp.zeros(out_ref.shape, jnp.float32)
    out_ref[0:1] = cross
    out_ref[1:2] = left
    out_ref[2:3] = right


def pair_coefs(cross, left_sq, right_sq):
    return 1.0 - cross / (2.0 * (left_sq + epsilon)), 1.0 - cross / (2.0 * (right_sq + epsilon))


def sum_four(refs):
    return (refs[0][...] + refs[1][...]) + (refs[2][...] + refs[3][...])


def pair_mix_kernel(pieces, s_ref, t0, t1, t2, t3, keep_ref, received_ref, *out_refs):
    core = s_ref[0]
    totals = jnp.sum(sum_four((t0, t1, t2, t3)), axis=1, keepdims=True)
    left, right = pair_coefs(totals[0:1], totals[1:2], totals[2:3])
    keep_coef = jnp.where(core == 0, left, right)
    received_coef = jnp.where(core == 0, right, left)
    for d, out in enumerate(out_refs[:pieces]):
        out[...] = keep_coef * keep_ref[d] + received_coef * received_ref[d]
    for out in out_refs[pieces:]:
        out[...] = jnp.zeros(out.shape, jnp.float32)
        out[0:1] = jnp.broadcast_to(keep_coef, (1, out.shape[1]))
        out[1:2] = jnp.broadcast_to(received_coef, (1, out.shape[1]))


def gram_kernel(s_ref, *refs):
    upper, x = s_ref[0], s_ref[1]
    coefs, own, other, gram_ref, late_ref = refs[7:]
    late_ref[...] = coefs[0:1] * own[...] + coefs[1:2] * other[...]
    blocks = refs[:7] + (late_ref,)
    node = [2 * jnp.bitwise_xor(upper, d // 2) + jnp.bitwise_xor(x, d % 2) for d in range(4)]
    for e in range(4):
        for d in range(e + 1):
            value = sum(column_sums(blocks[slot_of(d, dy)][...], blocks[slot_of(e, dy)][...]) for dy in range(2))
            gram_ref[pl.ds(4 * node[d] + node[e], 1)] = value
            gram_ref[pl.ds(4 * node[e] + node[d], 1)] = value


def slot_of(d, dy):
    index = 2 * dy + d % 2
    return 7 - index if d // 2 else index


def place_kernel(s_ref, *refs):
    upper, x, y = s_ref[0], s_ref[1], s_ref[2]
    blocks, (out_ref, rows_ref) = refs[4:12], refs[12:]
    gram = jnp.sum(sum_four(refs[:4]), axis=1, keepdims=True)
    g = lambda a, b: gram[4 * a + b : 4 * a + b + 1]
    p = pair_coefs(g(0, 1), g(0, 0), g(1, 1)) + pair_coefs(g(2, 3), g(2, 2), g(3, 3))
    cross = p[0] * (p[2] * g(0, 2) + p[3] * g(0, 3)) + p[1] * (p[2] * g(1, 2) + p[3] * g(1, 3))
    near = p[0] * p[0] * g(0, 0) + 2.0 * p[0] * p[1] * g(0, 1) + p[1] * p[1] * g(1, 1)
    far = p[2] * p[2] * g(2, 2) + 2.0 * p[2] * p[3] * g(2, 3) + p[3] * p[3] * g(3, 3)
    near_coef, far_coef = pair_coefs(cross, near, far)
    absolute = (near_coef * p[0], near_coef * p[1], far_coef * p[2], far_coef * p[3])
    coefs = []
    for d in range(4):
        owner = 2 * jnp.bitwise_xor(upper, d // 2) + jnp.bitwise_xor(x, d % 2)
        coef = absolute[3]
        for a in range(3):
            coef = jnp.where(owner == a, absolute[a], coef)
        coefs.append(coef)
    for dy in range(2):
        part = [blocks[slot_of(d, dy)][...] for d in range(4)]
        block = coefs[0] * part[0] + coefs[1] * part[1] + (coefs[2] * part[2] + coefs[3] * part[3])
        upper_half = pltpu.roll(block, HALF, 1)
        rows = jnp.concatenate([block[:, :HALF], upper_half[:, :HALF]], axis=0)
        rows = rows.reshape(rows_ref.shape[0], HALF, HALF)
        slot = jnp.bitwise_xor(y, dy)
        for k in range(rows_ref.shape[0]):
            rows_ref[k, slot] = rows[k]
    out_ref[...] = rows_ref[...].reshape(out_ref.shape[1], HALF).T


VM = pl.BlockSpec(memory_space=pltpu.VMEM)
HB = pl.BlockSpec(memory_space=pltpu.HBM)
SM = pl.BlockSpec(memory_space=pltpu.SMEM)


def f32(*shape):
    return jax.ShapeDtypeStruct(shape, jnp.float32)


def tile_plan(images, targets, weight):
    return tiles(images, targets, weight)


def tiles(images, targets, weight):
    imgs, side, _, channels = images.shape
    width = channels // 2
    rows = side * side * imgs
    node_id = lax.axis_index("node")
    local_id = lax.axis_index("local")
    z, c = node_id // 2, node_id % 2
    y, x = local_id // 2, local_id % 2

    def scalars(*values):
        return jnp.stack([jnp.asarray(v, jnp.int32) for v in values])

    xt = jnp.transpose(images, (1, 2, 0, 3))
    x_own, x_other = pl.pallas_call(
        split_kernel,
        out_shape=(f32(rows, width), f32(rows, width)),
        in_specs=[SM, HB],
        out_specs=(VM, VM),
        scratch_shapes=[
            pltpu.VMEM((side, rows // side, channels), jnp.float32),
            pltpu.SemaphoreType.DMA((side,)),
        ],
        compiler_params=pltpu.CompilerParams(vmem_limit_bytes=ALONE),
        name="split_images",
    )(scalars(y), xt.reshape(rows, channels))
    x_y = hop(x_other, lambda z, c, y, x: (z, c, 1 - y, x))
    x_x = hop(x_own, lambda z, c, y, x: (z, c, y, 1 - x))
    x_d = hop(x_other, lambda z, c, y, x: (z, c, 1 - y, 1 - x))

    tt = jnp.transpose(targets, (1, 2, 0, 3)).reshape(rows, channels)
    taps = weight.shape[0] * weight.shape[1]
    own_far, other_far, own_near, other_near = pl.pallas_call(
        residual_kernel,
        out_shape=(f32(rows, 128),) * 4,
        in_specs=[SM] + [HB] * 3,
        out_specs=(VM,) * 4,
        scratch_shapes=[
            pltpu.VMEM((rows, channels), jnp.float32),
            pltpu.VMEM((rows, channels), jnp.float32),
            pltpu.VMEM((taps, channels, channels), jnp.float32),
            pltpu.VMEM((rows, 3 * channels), jnp.bfloat16),
            pltpu.VMEM((side + 2, side + 2, imgs, channels), jnp.float32),
            pltpu.SemaphoreType.DMA((2,)),
            pltpu.SemaphoreType.DMA((taps,)),
        ],
        cost_estimate=pl.CostEstimate(
            flops=6 * rows * taps * channels * channels, bytes_accessed=4 * taps * channels * channels, transcendentals=0
        ),
        compiler_params=pltpu.CompilerParams(vmem_limit_bytes=ALONE),
        name="residual",
    )(scalars(x, z // 2), xt.reshape(rows, channels), tt, weight.reshape(taps, channels, channels))
    far = exchange(own_far, other_far)
    near = exchange(own_near, other_near)

    span = (side + 1) * 4 * imgs
    xt_shape = (side, width, 2 * span)
    images_t, *own_pieces = pl.pallas_call(
        lambda *refs: prepare_kernel(side, *refs),
        out_shape=(jax.ShapeDtypeStruct(xt_shape, jnp.bfloat16),) + (f32(rows, 128),) * 2,
        in_specs=[VM] * 6,
        out_specs=(VM,) * 3,
        compiler_params=pltpu.CompilerParams(vmem_limit_bytes=SHARED),
        name="prepare",
    )(x_own, x_x, x_y, x_d, own_far, own_near)
    far, near = (own_pieces[0], *far[1:]), (own_pieces[1], *near[1:])

    z_count = lax.axis_size("node") // 2
    part = taps * width // 8
    count = 2 * z_count
    half = count // 2
    place = scalars(z // 2, x, y)

    def gradient(pieces, early, flip):
        return pl.pallas_call(
            lambda *refs: gradient_kernel(1.0 / rows, side, *refs),
            out_shape=(f32(half, part, 128),) * 2 + (f32(part, 128),) * early,
            in_specs=[SM] + [VM] * 5,
            out_specs=(VM,) * (2 + early),
            scratch_shapes=[
                pltpu.VMEM((side, side + 3, 4 * imgs, 128), jnp.bfloat16),
                pltpu.VMEM((side, side + 3, 4 * imgs, 128), jnp.bfloat16),
                pltpu.VMEM((taps * width // BLK, BLK, 128), jnp.float32),
            ],
            cost_estimate=pl.CostEstimate(
                flops=24 * rows * taps * width * 128, bytes_accessed=4 * taps * width * 128, transcendentals=0
            ),
            compiler_params=pltpu.CompilerParams(vmem_limit_bytes=SHARED),
        )(scalars(c, y ^ flip, z % 2 ^ flip), images_t, *pieces)

    def dots(keep, received, before):
        return pl.pallas_call(
            pair_dots_kernel,
            out_shape=f32(8, 128),
            in_specs=[SM, VM, VM] + [VM] * len(before),
            out_specs=VM,
            compiler_params=pltpu.CompilerParams(vmem_limit_bytes=SHARED),
        )(scalars(c), keep, received, *before)

    across = lambda z, c, y, x: (z, 1 - c, y, x)
    keep_far, send_far, early_keep, early_send = gradient(far, 2, 1)
    received_far = hop(send_far, across)
    last = half - 1
    early_own = hop(early_keep, mover(count - 1))
    early_other = hop(early_send, lambda z, c, y, x: mover(count - 1)(z, 1 - c, y, x))
    keep_near, send_near = gradient(near, 0, 0)
    received_near = hop(send_near, across)
    totals = dots(keep_far, received_far, ())
    totals = plane_sum(dots(keep_near, received_near, (totals,)))

    def mix(keep, received, pieces):
        return pl.pallas_call(
            lambda *refs: pair_mix_kernel(pieces, *refs),
            out_shape=(f32(part, 128),) * pieces + (f32(8, 128),) * (half - pieces),
            in_specs=[SM] + [VM] * 6,
            out_specs=(VM,) * half,
            compiler_params=pltpu.CompilerParams(vmem_limit_bytes=SHARED),
        )(scalars(c), *totals, keep, received)

    mixed_far = mix(keep_far, received_far, last)
    blocks = tuple(mix(keep_near, received_near, half)) + tuple(mixed_far)

    moved = [hop(blocks[index], mover(index)) for index in range(count)]
    gram, moved[-1] = pl.pallas_call(
        gram_kernel,
        out_shape=(f32(16, 128), f32(part, 128)),
        in_specs=[SM] + [VM] * (count + 2),
        out_specs=(VM, VM),
        compiler_params=pltpu.CompilerParams(vmem_limit_bytes=SHARED),
        name="gram",
    )(place, *moved, early_own, early_other)
    along = [hop(gram, lambda z, c, y, x, d=d: (z ^ d, c, y, x)) for d in range(1, z_count)]
    gram = plane_sum((gram + along[0]) + (along[1] + along[2]))
    out = pl.pallas_call(
        place_kernel,
        out_shape=f32(HALF, 4 * part),
        in_specs=[SM] + [VM] * (4 + count),
        out_specs=VM,
        scratch_shapes=[pltpu.VMEM((2 * part // HALF, 2, HALF, HALF), jnp.float32)],
        compiler_params=pltpu.CompilerParams(vmem_limit_bytes=SHARED),
        name="place",
    )(place, *gram, *moved)
    return out.T


def mover(index):
    e = index // 4
    index = 7 - index if e else index
    dy, dx = index // 2, index % 2
    return lambda z, c, y, x: (2 * (z // 2 ^ e) + c, x, y ^ dy, z % 2 ^ dx)


def exchange(own, other):
    along_x = hop(other, lambda z, c, y, x: (z, c, y, 1 - x))
    across = hop(other, lambda z, c, y, x: (z, c, 1 - y, 1 - x))
    along_y = hop(own, lambda z, c, y, x: (z, c, 1 - y, x))
    return own, along_x, along_y, across


def plane_sum(value):
    value = value + hop(value, lambda z, c, y, x: (z, 1 - c, y, x))
    across = [hop(value, lambda z, c, y, x, d=d: (z, c, y ^ (d >> 1), x ^ (d & 1))) for d in (1, 2, 3)]
    return [value] + across


def fits(images, mesh):
    return (
        mesh.shape["local"] == 4
        and mesh.shape["node"] == 8
        and images.shape[3] == mesh.shape["node"] * HALF
        and images.shape[0] // mesh.size == 8
    )


def solution(mesh):
    def run(images, targets, weight):
        tiled = fits(images, mesh)
        step = jax.shard_map(
            tile_plan if tiled else general_plan,
            mesh=mesh,
            in_specs=(
                P(("node", "local"), None, None, None),
                P(("node", "local"), None, None, None),
                P(),
            ),
            out_specs=P("local", "node"),
            check_vma=False,
        )
        return step(images, targets, weight)

    return run
```
